512 devices in a mesh: bins: 128 (over z, y, core), scans: 4 (over x).
Axes of the slice: x: 4, y: 8, z: 8, core: 2. Of those that a mesh axis runs over, the one named last changes fastest.
Arguments:
- profiles: float32 [4, 4194304], P('scans', 'bins'), may hold values from -150 to 150
- band_edges: int32 [6], replicated, may hold values from 0 to 4096, as said below
- owner_counts: int32 [128], replicated, may hold values from 1 to 64, 4096 in all
- dynamics: float32 [5, 64, 64], replicated, may hold values from -0.6 to 0.6
- prev_state: float32 [8192, 4, 128], P('bins', 'scans'), may hold values from -6 to 6
Outputs:
- new_state: float32 [8192, 4, 128], P('bins', 'scans')
The draws below stay inside these ranges and needn't reach their ends.
Inputs may be any that keep to these rules, and one draw needn't show every extreme that they name: Strictly increasing, band_edges[0] = 0 and band_edges[5] = 4096. `owner_counts`: the counts sum to 4096, and some owner holds exactly 64 tiles.
All inputs are finite; a program needn't handle non-finite values.
Results may differ from the reference program's by a relative error of at most 0.0001.
Values sent between devices are 32-bit elements; how exact they have to be, the bound alone decides.
A program may use at most 64 MiB of HBM per device.

```python
import math
import jax
import jax.numpy as jnp
import numpy as np
from jax import lax

NBINS = 4194304
PROFILES = 4
TILE = 512
STATES = 64
NCLASS = 5
NT = 4096
CAP = 64
SLOTS = 8192
N_BINS = 128


def draw_profiles(key, part):
    key_scale = jax.random.fold_in(key, 11)
    key_noise = jax.random.fold_in(key, 12)
    row_index = jnp.arange(PROFILES, dtype=jnp.float32)
    trend_scale = jnp.exp(jnp.log(3.0) * row_index / max(PROFILES - 1, 1))
    jitter = jnp.exp(jax.random.uniform(key_scale, (PROFILES,), jnp.float32, 0.0, jnp.log(10.0)))
    scaling = trend_scale * jitter
    values = jnp.clip(jax.random.normal(key_noise, (PROFILES, NBINS), jnp.float32), -5.0, 5.0)
    return (scaling[:, None] * values).astype(jnp.float32)


def draw_band_edges(key, part):
    interior = jax.random.permutation(jax.random.fold_in(key, 21), NT - 1)[:NCLASS - 1] + 1
    interior = jnp.sort(interior.astype(jnp.int32))
    return jnp.concatenate([jnp.zeros((1,), jnp.int32), interior, jnp.full((1,), NT, jnp.int32)])


def shard_levels(own_key, dims, cuts, smallest, largest):
    factor_of = 1.0
    for axis_at, blocks in cuts:
        heights = jax.random.uniform(jax.random.fold_in(jax.random.fold_in(own_key, 6), axis_at), (blocks,), jnp.float32, smallest / len(cuts), largest / len(cuts))
        factor_of = factor_of * jnp.repeat(jnp.exp(heights), dims[axis_at] // blocks).reshape((-1,) + (1,) * (len(dims) - 1 - axis_at))
    return factor_of


def profile(number_of, total, reach, lean):
    loads = [(1 << 20) // math.isqrt(standing ** lean) + 1 for standing in range(2, number_of + 1)]
    spare, given = total - reach - (number_of - 1), [1] * (number_of - 1)
    while spare > 0:
        free = [i for i in range(number_of - 1) if given[i] < reach]
        mass, budget = sum([loads[i] for i in free]), spare
        for i in free:
            addition = min(reach - given[i], max(1, budget * loads[i] // mass), spare)
            given[i] = given[i] + addition
            spare = spare - addition
    return np.array([reach] + given)


def ragged_sizes(rng, count, total, reach, lean):
    if count == 2:
        one = jax.random.randint(rng, (), max(1, total - reach), min(reach, total - 1) + 1)
        return jnp.stack([one, total - one])
    sizes = jnp.asarray(profile(count, total, reach, lean), jnp.int32)
    twos = (count - 1) // 2
    donor, taker = sizes[1:1 + 2 * twos:2], sizes[2:2 + 2 * twos:2]
    slack = jnp.minimum(donor - 1, reach - taker)
    passed = jax.random.randint(jax.random.fold_in(rng, 1), (twos,), 0, 1 << 20) % (slack + 1)
    sizes = sizes.at[1:1 + 2 * twos:2].set(donor - passed).at[2:2 + 2 * twos:2].set(taker + passed)
    return sizes[jax.random.permutation(jax.random.fold_in(rng, 2), count)]


def scatter_about(stream_key, shape, spread, most, split=(), kind=jnp.bfloat16):
    values = spread * jax.random.normal(stream_key, shape, jnp.float32)
    if split:
        values = values * shard_levels(stream_key, shape, split, -0.22, 0.18)
    return jnp.clip(values, -most, most).astype(kind)


def setup_inputs(seed: int = 0) -> dict:
    streams_of = jax.random.split(jax.random.key(seed), 6)
    profiles = draw_profiles(jax.random.fold_in(streams_of[5], 71), 0)
    band_edges = draw_band_edges(jax.random.fold_in(streams_of[5], 71), 0)
    owner_counts = ragged_sizes(streams_of[2], N_BINS, NT, CAP, 2).astype(jnp.int32)
    dynamics = scatter_about(streams_of[3], (NCLASS, STATES, STATES), 0.15, 0.6, (), jnp.float32)
    prev_state = scatter_about(streams_of[4], (SLOTS, PROFILES, 2 * STATES), 1.0, 6.0, ((0, 128), (1, 4)), jnp.float32)
    return dict(profiles=profiles, band_edges=band_edges, owner_counts=owner_counts, dynamics=dynamics, prev_state=prev_state)


EPSILON = 1e-05
HIGHEST = lax.Precision.HIGHEST

def tile_sums(profile_row):
    spectrum = jnp.fft.rfft(profile_row)[:NBINS // 2]
    real_part = jnp.real(spectrum).reshape(NT, STATES, TILE // STATES)
    imag_part = jnp.imag(spectrum).reshape(NT, STATES, TILE // STATES)
    bin_power = lax.optimization_barrier(jnp.sum(real_part * real_part + imag_part * imag_part, axis=(1, 2)))
    return (lax.optimization_barrier(jnp.sum(real_part, axis=2)), lax.optimization_barrier(jnp.sum(imag_part, axis=2)), bin_power)

def measure(fine_sums, mean_power, band_index):
    measured = jnp.zeros_like(fine_sums)
    for class_index in range(NCLASS):
        group_span = 2 ** class_index
        state_count = STATES // group_span
        coarse = lax.optimization_barrier(jnp.sum(fine_sums.reshape(fine_sums.shape[:-1] + (state_count, group_span)), axis=-1))
        coarse = jnp.pad(coarse, [(0, 0)] * (coarse.ndim - 1) + [(0, STATES - state_count)])
        scaling = 1.0 / jnp.sqrt(TILE // state_count * (mean_power + EPSILON))
        chosen = band_index == class_index
        measured = measured + jnp.where(chosen[:, None, None, None], coarse * scaling[:, None, None, None], 0.0)
    return measured

def update(dynamics, band_index, previous, measured, occupied):
    state_index = jnp.arange(STATES)
    blocks = []
    for class_index in range(NCLASS):
        state_count = STATES // 2 ** class_index
        inside = state_index < state_count
        blocks.append(jnp.where(inside[:, None] & inside[None, :], dynamics[class_index], 0.0))
    masked = jnp.stack(blocks)
    selection = (band_index[:, None] == jnp.arange(NCLASS)[None, :]).astype(masked.dtype)
    picked = jnp.einsum('rk,kij->rij', selection, masked, precision=HIGHEST)
    updated = jnp.einsum('rij,rpcj->rpci', picked, previous, precision=HIGHEST) + measured
    return jnp.where(occupied[:, None, None, None], updated, 0.0)

def reference(profiles, band_edges, owner_counts, dynamics, prev_state):
    fine_real, fine_imag, bin_power = lax.map(tile_sums, profiles)
    mean_power = lax.optimization_barrier(jnp.sum(bin_power, axis=0)) / (PROFILES * TILE)
    stacked = jnp.stack([fine_real, fine_imag], axis=2)
    fine_all = jnp.transpose(stacked, (1, 0, 2, 3))
    tile_numbers = jnp.arange(NT, dtype=jnp.int32)
    band_all = lax.optimization_barrier(jnp.sum((tile_numbers[:, None] >= band_edges[None, 1:NCLASS]).astype(jnp.int32), axis=1))
    measured_all = measure(fine_all, mean_power, band_all)
    starts = jnp.cumsum(owner_counts) - owner_counts
    slot_index = jnp.arange(CAP, dtype=jnp.int32)
    wanted = (starts[:, None] + slot_index[None, :]).reshape(SLOTS)
    occupied = (slot_index[None, :] < owner_counts[:, None]).reshape(SLOTS)
    slot_tiles = jnp.clip(wanted, 0, NT - 1).astype(jnp.int32)
    measured = measured_all[slot_tiles]
    band_index = band_all[slot_tiles]
    previous = prev_state.reshape(SLOTS, PROFILES, 2, STATES)
    updated = update(dynamics, band_index, previous, measured, occupied)
    return updated.reshape(SLOTS, PROFILES, 2 * STATES)
```

```python
import functools

import jax
import jax.numpy as jnp
import ml_dtypes
import numpy as np
from jax import lax
from jax.experimental import pallas as pl
from jax.experimental.pallas import tpu as pltpu
from jax.sharding import PartitionSpec as P

MESH = pl.DeviceIdType.MESH
BF=jnp.bfloat16; F32=jnp.float32
ND=128; NB=1<<22; M=1<<15; EPS=1e-5; NCLASS=5

def pair(a):
    a=np.asarray(a,np.float64)
    hi=a.astype(np.float32).astype(ml_dtypes.bfloat16)
    lo=(a-hi.astype(np.float64)).astype(np.float32).astype(ml_dtypes.bfloat16)
    return hi,lo
def split(x):
    hi=x.astype(BF); lo=(x-hi.astype(F32)).astype(BF)
    return hi,lo
def dot(a,b): return lax.dot_general(a,b,(((1,),(0,)),((),())),preferred_element_type=F32)
def dot_nt(a,b): return lax.dot_general(a,b,(((1,),(1,)),((),())),preferred_element_type=F32)
def dot3(a,b,d=dot):
    return d(a[0],b[0])+(d(a[0],b[1])+d(a[1],b[0]))
def tables():
    i=np.arange(128)[:,None]; j=np.arange(128)[None,:]; a=np.arange(256)[None,:]
    ang=2*np.pi*(i*j%128)/128; C,S=np.cos(ang),np.sin(ang)
    F1=np.concatenate([C,-S],0)
    MM=np.block([[C,S],[-S,C]])
    ang=2*np.pi*(i*a%256)/256; C2,S2=np.cos(ang),np.sin(ang)
    W2=np.block([[C2,S2],[-S2,C2]])
    ang=2*np.pi*(i*a)/M
    tw=np.stack([np.cos(ang),-np.sin(ang)]).astype(np.float32)
    b=np.arange(128)
    G=np.zeros((128,128))
    G[b,b//8]=1
    for m in range(16):
        g=15-m
        for bb in range(8*g+1,min(8*g+9,128)): G[bb,16+m]=1
    place=np.zeros((5,128,256))
    for q in range(5):
        for m in range(16):
            if q<4:
                place[q,m,16*q+m]=1; place[q,64+m,64+16*q+m]=1
                place[q,16+m,48-16*q+m]=1; place[q,80+m,64+48-16*q+m]=-1
        if q<4:
            place[q,40,128]=1; place[q,41,128]=1
        if q>=1:
            place[q,42,128]=1; place[q,32,64-16*q]=1; place[q,96,128-16*q]=-1
    place=place.reshape(640,256)
    co=np.zeros((5,128,128))
    for be in range(5):
        for k in range(64):
            co[be,k,k>>be]=1; co[be,64+k,64+(k>>be)]=1
    co=co.reshape(640,128)
    return dict(F1=pair(F1),MM=pair(MM),W2=pair(W2),tw=tw,G=G.astype(ml_dtypes.bfloat16),place=place.astype(ml_dtypes.bfloat16),co=co.astype(ml_dtypes.bfloat16))

def iota(shape,d): return lax.broadcasted_iota(jnp.int32,shape,d)

def stage1(R1, F1, W2, tw):
    A=dot3(F1, split(R1))
    Ar,Ai=A[:128],A[128:]
    tr,ti=tw[0],tw[1]
    Br=Ar*tr-Ai*ti; Bi=Ar*ti+Ai*tr
    B=jnp.concatenate([Br,Bi],1)
    Y=dot3(W2, split(B), dot_nt)
    Yr,Yi=Y[:128],Y[128:]
    lane=iota((1,256),1)
    nyq=jnp.sum(jnp.where(lane%2==0,Br[0:1],-Br[0:1]),axis=1,keepdims=True)
    first=(iota((128,128),0)==0)&(iota((128,128),1)==0)
    Yi=jnp.where(first,nyq,Yi)
    return jnp.concatenate([Yr,Yi],1)

def twiddle(me):
    n=iota((128,128),0); b=iota((128,128),1)
    th=(n*(128*me+b)).astype(F32)*(2*np.pi/NB)
    nn=n.astype(F32)*(2*np.pi/256)
    zero=me==0
    return jnp.cos(th),jnp.sin(th),jnp.cos(nn),jnp.sin(nn)

def stage2(R2, me, T, MM, G):
    Tr,Ts,Nr,Ns=T
    Rr,Ri=R2[:,:128],R2[:,128:]
    lane0=iota((128,128),1)==0
    zero=me==0
    Ri0=jnp.where(lane0&zero,0.0,Ri)
    Yr=Rr*Tr+Ri0*Ts; Yi=Ri0*Tr-Rr*Ts
    Er=jnp.where(zero,Ri*Nr,Yr); Ei=jnp.where(zero,-Ri*Ns,Yi)
    Y=jnp.concatenate([Yr,Yi],0); E=jnp.concatenate([Er,Ei],0)
    yh,yl=split(Y)
    Z=dot(yh,G)+dot(yl,G)
    Z=jnp.where(iota((256,128),1)==32,E[:,0:1],Z)
    zh,zl=split(Z)
    X=dot3(MM,(jnp.concatenate([yh,zh],1),jnp.concatenate([yl,zl],1)))
    Xr,Xi=X[:128,:128],X[128:,:128]; Fr,Fi=X[:128,128:],X[128:,128:]
    rows=iota((128,128),0)
    Pw=Xr*Xr+Xi*Xi
    Pw=jnp.where(lane0&(rows>=64),0.0,Pw)
    ps=jnp.sum(Pw,axis=1,keepdims=True)
    Pe=(Fr*Fr+Fi*Fi)
    lane=iota((128,128),1)
    Q=jnp.where(lane==0,ps,jnp.where(lane==32,Pe,0.0))
    Qt=jnp.transpose(Q)
    return Fr,Fi,Qt

def starts_of(counts_row):
    o=iota((128,128),0); k=iota((128,128),1)
    return jnp.sum(jnp.where(k<o,counts_row.astype(F32),0.0),axis=1,keepdims=True).astype(jnp.int32)

def onehots(starts, me):
    q4=me//4
    k=iota((128,128),1)
    def row(cl):
        return (starts+((cl-starts)&63))>>6
    main=row(q4); mir=127-row(63-q4); ext=127-row(63-((me+127)%128)//4)
    Sm=(k==main)&(k<64); Sx=(k==mir)&(k>=64); Se=(k==ext)&(k>=64)
    return Sm,Sx,Se

def stage3(Fr,Fi,S):
    Sm,Sx,Se=S
    rows=iota((128,128),0); lane=iota((128,128),1)
    keep=((rows<64)&(lane<16))|((rows>=64)&(lane>=16)&(lane<32))
    keepe=(rows>=64)&(lane==32)
    Wm=jnp.concatenate([jnp.where(keep,Fr,0.0),jnp.where(keep,Fi,0.0)],1)
    We=jnp.concatenate([jnp.where(keepe,Fr,0.0),jnp.where(keepe,Fi,0.0)],1)
    W=jnp.concatenate([Wm,We],0)
    SS=jnp.concatenate([(Sm|Sx).astype(F32).astype(BF),Se.astype(F32).astype(BF)],1)
    h,l=split(W)
    Ms=dot(SS,h)+dot(SS,l)
    return Ms[:,:128], Ms[:,128:]

def stage3b(mr,mi_rolled,S,tot):
    Sm,Sx,Se=S
    p0=tot[0:1]; p1=tot[1:2]
    z=0.0
    a=jnp.sum(jnp.where(Sm,p0,z),axis=1,keepdims=True)
    b=jnp.sum(jnp.where(Sx,p0,z),axis=1,keepdims=True)
    c=jnp.sum(jnp.where(Se,p1,z),axis=1,keepdims=True)
    lane=iota((128,128),1)
    return jnp.where(lane<40,mr,jnp.where(lane>=64,mi_rolled,jnp.where(lane==40,a,jnp.where(lane==41,b,jnp.where(lane==42,c,0.0)))))

def slot_info(counts_row, edges, me):
    k=iota((64,128),1)
    st=jnp.sum(jnp.where(k<me,counts_row.astype(F32),0.0),axis=1,keepdims=True).astype(jnp.int32)
    cn=jnp.sum(jnp.where(k==me,counts_row.astype(F32),0.0),axis=1,keepdims=True).astype(jnp.int32)
    s=iota((64,1),0)
    t=st+s
    band=sum([(t>=edges[e]).astype(jnp.int32) for e in range(1,5)])
    return t,band,s<cn

def owner_select(t):
    c=t&63; main=c<32
    j=iota((64,128),1)
    r4=4*jnp.where(main,c,63-c)
    sel=[(j==r4+q).astype(F32).astype(BF) for q in range(4)]
    sel.append((j==((4*(64-c))&127)).astype(F32).astype(BF))
    return jnp.concatenate(sel,0)

def state_part(prev, dyn, t, band):
    pr=jnp.concatenate([prev[:,:64],prev[:,64:]],0)
    band2=jnp.concatenate([band,band],0)
    cnt=64>>band2
    lane=iota((128,64),1)
    pr=jnp.where(lane<cnt,pr,0.0)
    out=jnp.zeros((128,64),F32)
    for be in range(NCLASS):
        x=jnp.where(band2==be,pr,0.0)
        out=out+dot3(split(x),split(dyn[be]),dot_nt)
    out=jnp.where(lane<cnt,out,0.0)
    return jnp.concatenate([out[:64],out[64:]],1)

def stage4(R3, sel, t, band, occ, place, co, spart):
    h,l=split(R3)
    main=(t&63)<32
    lane=iota((64,128),1)
    inmain=(lane<16)|((lane>=64)&(lane<80))|(lane==40)
    inmir=((lane>=16)&(lane<32))|((lane>=80)&(lane<96))|(lane==41)
    inext=(lane==32)|(lane==96)|(lane==42)
    res=None
    for v in (h,l):
        T=dot(sel,v)
        parts=[]
        for q in range(5):
            mk=(main&inmain&(q<4))|(jnp.logical_not(main)&((inmir&(q<4))|(inext&(q>=1))))
            parts.append(jnp.where(mk,T[64*q:64*q+64],0.0).astype(BF))
        o=dot(jnp.concatenate(parts,1),place)
        res=o if res is None else res+o
    fine=res[:,:128]; pw=res[:,128:129]
    fh,fl=split(fine)
    meas=None
    for v in (fh,fl):
        x=jnp.concatenate([jnp.where(band==be,v.astype(F32),0.0).astype(BF) for be in range(5)],1)
        o=dot(x,co)
        meas=o if meas is None else meas+o
    mp=pw/(4*512)
    scale=1.0/jnp.sqrt((8<<band).astype(F32)*(mp+EPS))
    st=iota((64,128),1)&63
    meas=jnp.where(st<(64>>band),meas*scale,0.0)
    return jnp.where(occ,meas+spart,0.0)


def kernel(edges_ref, x_h, cnt_h, dyn_h, prev_h, f1h_h, f1l_h, mmh_h, mml_h, w2h_h, w2l_h, tw_h, g_h, pl_h, co_h,
           o_ref,
           x_v, cnt_v, dyn_v, prev_v, f1h_v, f1l_v, mmh_v, mml_v, w2h_v, w2l_v, tw_v, g_v, pl_v, co_v,
           s1, r1, s2, r2, s3, r3, xs, xr, dummy, t_v, oh_v, sp_v, sel_v, csem, sem):
    me = lax.axis_index("bins")
    mx = lax.axis_index("scans")
    hs = [x_h, cnt_h, dyn_h, prev_h, f1h_h, f1l_h, mmh_h, mml_h, w2h_h, w2l_h, tw_h, g_h, pl_h, co_h]
    vs = [x_v, cnt_v, dyn_v, prev_v, f1h_v, f1l_v, mmh_v, mml_v, w2h_v, w2l_v, tw_v, g_v, pl_v, co_v]
    loads = [pltpu.make_async_copy(h, v, csem.at[i]) for i, (h, v) in enumerate(zip(hs, vs))]
    loads[0].start()
    bar = pltpu.get_barrier_semaphore()

    def sig(i, c):
        pl.semaphore_signal(bar, inc=1, device_id={"bins": lax.rem(me + i, ND)}, device_id_type=MESH)
        return c

    lax.fori_loop(1, ND, sig, 0)
    for i in range(1, 4):
        pl.semaphore_signal(bar, inc=1, device_id={"scans": lax.rem(mx + i, 4)}, device_id_type=MESH)
    for ld in loads[1:]:
        ld.start()
    loads[0].wait()
    s1[...] = jnp.concatenate([jnp.transpose(x_v[0:128, :]), jnp.transpose(x_v[128:256, :])], 1)
    pl.semaphore_wait(bar, ND + 2)

    def send_all(s, r, k):
        def one(i, c):
            j = lax.rem(me + i, ND)
            pltpu.make_async_remote_copy(s.at[pl.ds(j, 1)], r.at[pl.ds(me, 1)], sem.at[k], sem.at[k + 1],
                                         device_id={"bins": j}, device_id_type=MESH).start()
            return c
        lax.fori_loop(1, ND, one, 0)

    def wait_all(w, k):
        d = dummy.at[:, :, pl.ds(0, w)]
        pltpu.make_async_copy(d, d, sem.at[k]).wait()

    send_all(s1, r1, 0)
    r1[pl.ds(me, 1), :] = s1[pl.ds(me, 1), :]
    for ld in loads[1:]:
        ld.wait()
    T = twiddle(me)
    for i in range(4):
        t_v[i] = T[i]
    counts = cnt_v[...]
    for i, m in enumerate(onehots(starts_of(counts), me)):
        oh_v[i] = m.astype(F32)
    edges = [edges_ref[i] for i in range(6)]
    t, band, occ = slot_info(counts, edges, me)
    sp_v[...] = state_part(prev_v[...], dyn_v, t, band)
    sel_v[...] = owner_select(t)
    wait_all(256, 1)
    wait_all(256, 0)

    s2[...] = stage1(r1[...], (f1h_v[...], f1l_v[...]), (w2h_v[...], w2l_v[...]), tw_v)
    send_all(s2, r2, 2)
    r2[pl.ds(me, 1), :] = s2[pl.ds(me, 1), :]
    wait_all(256, 3)
    wait_all(256, 2)

    Fr, Fi, Qt = stage2(r2[...], me, [t_v[i] for i in range(4)], (mmh_v[...], mml_v[...]), g_v[...])
    xs[...] = Qt[0:8]
    xs[1:2, :] = Qt[32:33]
    for i in range(1, 4):
        pltpu.make_async_remote_copy(xs, xr.at[mx], sem.at[4], sem.at[5],
                                     device_id={"scans": lax.rem(mx + i, 4)}, device_id_type=MESH).start()
    xr[mx] = xs[...]
    S = [oh_v[i] > 0.5 for i in range(3)]
    mr, mi = stage3(Fr, Fi, S)
    mi = pltpu.roll(mi, 64, 1)
    d = xr.at[pl.ds(0, 3)]
    pltpu.make_async_copy(d, d, sem.at[5]).wait()
    pltpu.make_async_copy(d, d, sem.at[4]).wait()
    tot = xr[0] + xr[1] + xr[2] + xr[3]
    s3[...] = stage3b(mr, mi, S, tot)
    send_all(s3, r3, 6)
    r3[pl.ds(me, 1), :] = s3[pl.ds(me, 1), :]
    wait_all(128, 7)
    wait_all(128, 6)
    t, band, occ = slot_info(cnt_v[...], edges, me)
    o_ref[...] = stage4(r3[...], sel_v[...], t, band, occ, pl_v[...], co_v[...], sp_v[...])


def body(profiles, band_edges, owner_counts, dynamics, prev_state):
    tb = tables()
    consts = [*tb["F1"], *tb["MM"], *tb["W2"], tb["tw"], tb["G"], tb["place"], tb["co"]]
    ins = [profiles.reshape(256, 128), owner_counts.reshape(1, 128), dynamics, prev_state.reshape(64, 128)]
    ins += [jnp.asarray(c) for c in consts]
    V = pltpu.VMEM
    out = pl.pallas_call(
        kernel,
        out_shape=jax.ShapeDtypeStruct((64, 128), F32),
        in_specs=[pl.BlockSpec(memory_space=pltpu.SMEM)] + [pl.BlockSpec(memory_space=pl.ANY)] * len(ins),
        out_specs=pl.BlockSpec(memory_space=V),
        scratch_shapes=[V(i.shape, i.dtype) for i in ins] + [
            V((128, 256), F32), V((128, 256), F32), V((128, 256), F32), V((128, 256), F32),
            V((128, 128), F32), V((128, 128), F32), V((8, 128), F32), V((4, 8, 128), F32),
            V((127, 1, 256), F32), V((4, 128, 128), F32), V((3, 128, 128), F32), V((64, 128), F32), V((320, 128), BF),
            pltpu.SemaphoreType.DMA((len(ins),)), pltpu.SemaphoreType.DMA((8,))],
        compiler_params=pltpu.CompilerParams(collective_id=0, has_side_effects=True),
    )(band_edges, *ins)
    return out.reshape(64, 1, 128)


def solution(mesh):
    return jax.shard_map(
        body,
        mesh=mesh,
        in_specs=(P("scans", "bins"), P(), P(), P(), P("bins", "scans", None)),
        out_specs=P("bins", "scans", None),
        check_vma=False,
    )
```

```python
import functools

import jax
import jax.numpy as jnp
import ml_dtypes
import numpy as np
from jax import lax
from jax.experimental import pallas as pl
from jax.experimental.pallas import tpu as pltpu
from jax.sharding import PartitionSpec as P

MESH = pl.DeviceIdType.MESH
BF=jnp.bfloat16; F32=jnp.float32
ND=128; NB=1<<22; M=1<<15; EPS=1e-5; NCLASS=5

def pair(a):
    a=np.asarray(a,np.float64)
    hi=a.astype(np.float32).astype(ml_dtypes.bfloat16)
    lo=(a-hi.astype(np.float64)).astype(np.float32).astype(ml_dtypes.bfloat16)
    return hi,lo
def split(x):
    hi=x.astype(BF); lo=(x-hi.astype(F32)).astype(BF)
    return hi,lo
def dot(a,b): return lax.dot_general(a,b,(((1,),(0,)),((),())),preferred_element_type=F32)
def dot_nt(a,b): return lax.dot_general(a,b,(((1,),(1,)),((),())),preferred_element_type=F32)
def dot3(a,b,d=dot):
    return d(a[0],b[0])+(d(a[0],b[1])+d(a[1],b[0]))
def tables():
    i=np.arange(128)[:,None]; j=np.arange(128)[None,:]; a=np.arange(256)[None,:]
    ang=2*np.pi*(i*j%128)/128; C,S=np.cos(ang),np.sin(ang)
    F1=np.concatenate([C,-S],0)
    MM=np.block([[C,S],[-S,C]])
    ang=2*np.pi*(i*a%256)/256; C2,S2=np.cos(ang),np.sin(ang)
    W2=np.block([[C2,S2],[-S2,C2]])
    ang=2*np.pi*(i*a)/M
    tw=np.stack([np.cos(ang),-np.sin(ang)]).astype(np.float32)
    b=np.arange(128)
    G=np.zeros((128,128))
    G[b,b//8]=1
    for m in range(16):
        g=15-m
        for bb in range(8*g+1,min(8*g+9,128)): G[bb,16+m]=1
    place=np.zeros((5,128,256))
    for q in range(5):
        for m in range(16):
            if q<4:
                place[q,m,16*q+m]=1; place[q,64+m,64+16*q+m]=1
                place[q,16+m,48-16*q+m]=1; place[q,80+m,64+48-16*q+m]=-1
        if q<4:
            place[q,40,128]=1; place[q,41,128]=1
        if q>=1:
            place[q,42,128]=1; place[q,32,64-16*q]=1; place[q,96,128-16*q]=-1
    place=place.reshape(640,256)
    co=np.zeros((5,128,128))
    for be in range(5):
        for k in range(64):
            co[be,k,k>>be]=1; co[be,64+k,64+(k>>be)]=1
    co=co.reshape(640,128)
    return dict(F1=pair(F1),MM=pair(MM),W2=pair(W2),tw=tw,G=G.astype(ml_dtypes.bfloat16),place=place.astype(ml_dtypes.bfloat16),co=co.astype(ml_dtypes.bfloat16))

def iota(shape,d): return lax.broadcasted_iota(jnp.int32,shape,d)

def stage1(R1, F1, W2, tw):
    A=dot3(F1, split(R1))
    Ar,Ai=A[:128],A[128:]
    tr,ti=tw[0],tw[1]
    Br=Ar*tr-Ai*ti; Bi=Ar*ti+Ai*tr
    B=jnp.concatenate([Br,Bi],1)
    Y=dot3(W2, split(B), dot_nt)
    Yr,Yi=Y[:128],Y[128:]
    lane=iota((1,256),1)
    nyq=jnp.sum(jnp.where(lane%2==0,Br[0:1],-Br[0:1]),axis=1,keepdims=True)
    first=(iota((128,128),0)==0)&(iota((128,128),1)==0)
    Yi=jnp.where(first,nyq,Yi)
    return jnp.concatenate([Yr,Yi],1)

def twiddle(me):
    n=iota((128,128),0); b=iota((128,128),1)
    th=(n*(128*me+b)).astype(F32)*(2*np.pi/NB)
    nn=n.astype(F32)*(2*np.pi/256)
    zero=me==0
    return jnp.cos(th),jnp.sin(th),jnp.cos(nn),jnp.sin(nn)

def stage2(R2, me, T, MM, G):
    Tr,Ts,Nr,Ns=T
    Rr,Ri=R2[:,:128],R2[:,128:]
    lane0=iota((128,128),1)==0
    zero=me==0
    Ri0=jnp.where(lane0&zero,0.0,Ri)
    Yr=Rr*Tr+Ri0*Ts; Yi=Ri0*Tr-Rr*Ts
    Er=jnp.where(zero,Ri*Nr,Yr); Ei=jnp.where(zero,-Ri*Ns,Yi)
    Y=jnp.concatenate([Yr,Yi],0); E=jnp.concatenate([Er,Ei],0)
    yh,yl=split(Y)
    Z=dot(yh,G)+dot(yl,G)
    Z=jnp.where(iota((256,128),1)==32,E[:,0:1],Z)
    zh,zl=split(Z)
    X=dot3(MM,(jnp.concatenate([yh,zh],1),jnp.concatenate([yl,zl],1)))
    Xr,Xi=X[:128,:128],X[128:,:128]; Fr,Fi=X[:128,128:],X[128:,128:]
    rows=iota((128,128),0)
    Pw=Xr*Xr+Xi*Xi
    Pw=jnp.where(lane0&(rows>=64),0.0,Pw)
    ps=jnp.sum(Pw,axis=1,keepdims=True)
    Pe=(Fr*Fr+Fi*Fi)
    lane=iota((128,128),1)
    Q=jnp.where(lane==0,ps,jnp.where(lane==32,Pe,0.0))
    Qt=jnp.transpose(Q)
    return Fr,Fi,Qt

def starts_of(counts_row):
    o=iota((128,128),0); k=iota((128,128),1)
    return jnp.sum(jnp.where(k<o,counts_row.astype(F32),0.0),axis=1,keepdims=True).astype(jnp.int32)

def onehots(starts, me):
    q4=me//4
    k=iota((128,128),1)
    def row(cl):
        return (starts+((cl-starts)&63))>>6
    main=row(q4); mir=127-row(63-q4); ext=127-row(63-((me+127)%128)//4)
    Sm=(k==main)&(k<64); Sx=(k==mir)&(k>=64); Se=(k==ext)&(k>=64)
    return Sm,Sx,Se

def stage3(Fr,Fi,S):
    Sm,Sx,Se=S
    rows=iota((128,128),0); lane=iota((128,128),1)
    keep=((rows<64)&(lane<16))|((rows>=64)&(lane>=16)&(lane<32))
    keepe=(rows>=64)&(lane==32)
    Wm=jnp.concatenate([jnp.where(keep,Fr,0.0),jnp.where(keep,Fi,0.0)],1)
    We=jnp.concatenate([jnp.where(keepe,Fr,0.0),jnp.where(keepe,Fi,0.0)],1)
    W=jnp.concatenate([Wm,We],0)
    SS=jnp.concatenate([(Sm|Sx).astype(F32).astype(BF),Se.astype(F32).astype(BF)],1)
    h,l=split(W)
    Ms=dot(SS,h)+dot(SS,l)
    return Ms[:,:128], Ms[:,128:]

def stage3b(mr,mi_rolled,S,tot):
    Sm,Sx,Se=S
    p0=tot[0:1]; p1=tot[1:2]
    z=0.0
    a=jnp.sum(jnp.where(Sm,p0,z),axis=1,keepdims=True)
    b=jnp.sum(jnp.where(Sx,p0,z),axis=1,keepdims=True)
    c=jnp.sum(jnp.where(Se,p1,z),axis=1,keepdims=True)
    lane=iota((128,128),1)
    return jnp.where(lane<40,mr,jnp.where(lane>=64,mi_rolled,jnp.where(lane==40,a,jnp.where(lane==41,b,jnp.where(lane==42,c,0.0)))))

def slot_info(counts_row, edges, me):
    k=iota((64,128),1)
    st=jnp.sum(jnp.where(k<me,counts_row.astype(F32),0.0),axis=1,keepdims=True).astype(jnp.int32)
    cn=jnp.sum(jnp.where(k==me,counts_row.astype(F32),0.0),axis=1,keepdims=True).astype(jnp.int32)
    s=iota((64,1),0)
    t=st+s
    band=sum([(t>=edges[e]).astype(jnp.int32) for e in range(1,5)])
    return t,band,s<cn

def owner_select(t):
    c=t&63; main=c<32
    j=iota((64,128),1)
    r4=4*jnp.where(main,c,63-c)
    sel=[(j==r4+q).astype(F32).astype(BF) for q in range(4)]
    sel.append((j==((4*(64-c))&127)).astype(F32).astype(BF))
    return jnp.concatenate(sel,0)

def state_part(prev, dyn, t, band):
    pr=jnp.concatenate([prev[:,:64],prev[:,64:]],0)
    band2=jnp.concatenate([band,band],0)
    cnt=64>>band2
    lane=iota((128,64),1)
    pr=jnp.where(lane<cnt,pr,0.0)
    out=jnp.zeros((128,64),F32)
    for be in range(NCLASS):
        x=jnp.where(band2==be,pr,0.0)
        out=out+dot3(split(x),split(dyn[be]),dot_nt)
    out=jnp.where(lane<cnt,out,0.0)
    return jnp.concatenate([out[:64],out[64:]],1)

def stage4(R3, sel, t, band, occ, place, co, spart):
    h,l=split(R3)
    main=(t&63)<32
    lane=iota((64,128),1)
    inmain=(lane<16)|((lane>=64)&(lane<80))|(lane==40)
    inmir=((lane>=16)&(lane<32))|((lane>=80)&(lane<96))|(lane==41)
    inext=(lane==32)|(lane==96)|(lane==42)
    res=None
    for v in (h,l):
        T=dot(sel,v)
        parts=[]
        for q in range(5):
            mk=(main&inmain&(q<4))|(jnp.logical_not(main)&((inmir&(q<4))|(inext&(q>=1))))
            parts.append(jnp.where(mk,T[64*q:64*q+64],0.0).astype(BF))
        o=dot(jnp.concatenate(parts,1),place)
        res=o if res is None else res+o
    fine=res[:,:128]; pw=res[:,128:129]
    fh,fl=split(fine)
    meas=None
    for v in (fh,fl):
        x=jnp.concatenate([jnp.where(band==be,v.astype(F32),0.0).astype(BF) for be in range(5)],1)
        o=dot(x,co)
        meas=o if meas is None else meas+o
    mp=pw/(4*512)
    scale=1.0/jnp.sqrt((8<<band).astype(F32)*(mp+EPS))
    st=iota((64,128),1)&63
    meas=jnp.where(st<(64>>band),meas*scale,0.0)
    return jnp.where(occ,meas+spart,0.0)


def kernel(edges_ref, x_h, cnt_h, dyn_h, prev_h, f1h_h, f1l_h, mmh_h, mml_h, w2h_h, w2l_h, tw_h, g_h, pl_h, co_h,
           o_ref,
           x_v, cnt_v, dyn_v, prev_v, f1h_v, f1l_v, mmh_v, mml_v, w2h_v, w2l_v, tw_v, g_v, pl_v, co_v,
           s1, r1, s2, r2, s3, r3, xs, xr, dummy, t_v, oh_v, sp_v, sel_v, csem, sem):
    me = lax.axis_index("bins")
    mx = lax.axis_index("scans")
    hs = [x_h, cnt_h, dyn_h, prev_h, f1h_h, f1l_h, mmh_h, mml_h, w2h_h, w2l_h, tw_h, g_h, pl_h, co_h]
    vs = [x_v, cnt_v, dyn_v, prev_v, f1h_v, f1l_v, mmh_v, mml_v, w2h_v, w2l_v, tw_v, g_v, pl_v, co_v]
    loads = [pltpu.make_async_copy(h, v, csem.at[i]) for i, (h, v) in enumerate(zip(hs, vs))]
    loads[0].start()
    bar = pltpu.get_barrier_semaphore()

    z16, y2, c1 = me & 112, me & 14, me & 1
    ys = [((y2 + 2 * d) & 14) | (c1 ^ c) for d in (4, 3, 5, 2, 6, 1, 7, 0) for c in (1, 0)]

    def far_first(act):
        def ring(i, c):
            d = 4 + jnp.where((i & 1) == 1, -((i + 1) >> 1), i >> 1)
            zz = (z16 + 16 * d) & 112
            for y in ys:
                act(zz | y)
            return c
        lax.fori_loop(0, 7, ring, 0)
        for y in ys[:-1]:
            act(z16 | y)

    far_first(lambda j: pl.semaphore_signal(bar, inc=1, device_id={"bins": j}, device_id_type=MESH))
    for i in range(1, 4):
        pl.semaphore_signal(bar, inc=1, device_id={"scans": lax.rem(mx + i, 4)}, device_id_type=MESH)
    for ld in loads[1:]:
        ld.start()
    loads[0].wait()
    s1[...] = jnp.concatenate([jnp.transpose(x_v[0:128, :]), jnp.transpose(x_v[128:256, :])], 1)
    pl.semaphore_wait(bar, ND + 2)

    def send_all(s, r, k):
        def one(j):
            pltpu.make_async_remote_copy(s.at[pl.ds(j, 1)], r.at[pl.ds(me, 1)], sem.at[k], sem.at[k + 1],
                                         device_id={"bins": j}, device_id_type=MESH).start()
        far_first(one)

    def wait_all(w, k):
        d = dummy.at[:, :, pl.ds(0, w)]
        pltpu.make_async_copy(d, d, sem.at[k]).wait()

    send_all(s1, r1, 0)
    r1[pl.ds(me, 1), :] = s1[pl.ds(me, 1), :]
    for ld in loads[1:]:
        ld.wait()
    T = twiddle(me)
    for i in range(4):
        t_v[i] = T[i]
    counts = cnt_v[...]
    for i, m in enumerate(onehots(starts_of(counts), me)):
        oh_v[i] = m.astype(F32)
    edges = [edges_ref[i] for i in range(6)]
    t, band, occ = slot_info(counts, edges, me)
    sp_v[...] = state_part(prev_v[...], dyn_v, t, band)
    sel_v[...] = owner_select(t)
    wait_all(256, 1)
    wait_all(256, 0)

    s2[...] = stage1(r1[...], (f1h_v[...], f1l_v[...]), (w2h_v[...], w2l_v[...]), tw_v)
    send_all(s2, r2, 2)
    r2[pl.ds(me, 1), :] = s2[pl.ds(me, 1), :]
    wait_all(256, 3)
    wait_all(256, 2)

    Fr, Fi, Qt = stage2(r2[...], me, [t_v[i] for i in range(4)], (mmh_v[...], mml_v[...]), g_v[...])
    xs[...] = Qt[0:8]
    xs[1:2, :] = Qt[32:33]
    for i in range(1, 4):
        pltpu.make_async_remote_copy(xs, xr.at[mx], sem.at[4], sem.at[5],
                                     device_id={"scans": lax.rem(mx + i, 4)}, device_id_type=MESH).start()
    xr[mx] = xs[...]
    S = [oh_v[i] > 0.5 for i in range(3)]
    mr, mi = stage3(Fr, Fi, S)
    mi = pltpu.roll(mi, 64, 1)
    d = xr.at[pl.ds(0, 3)]
    pltpu.make_async_copy(d, d, sem.at[5]).wait()
    pltpu.make_async_copy(d, d, sem.at[4]).wait()
    tot = xr[0] + xr[1] + xr[2] + xr[3]
    s3[...] = stage3b(mr, mi, S, tot)
    send_all(s3, r3, 6)
    r3[pl.ds(me, 1), :] = s3[pl.ds(me, 1), :]
    wait_all(128, 7)
    wait_all(128, 6)
    t, band, occ = slot_info(cnt_v[...], edges, me)
    o_ref[...] = stage4(r3[...], sel_v[...], t, band, occ, pl_v[...], co_v[...], sp_v[...])


def body(profiles, band_edges, owner_counts, dynamics, prev_state):
    tb = tables()
    consts = [*tb["F1"], *tb["MM"], *tb["W2"], tb["tw"], tb["G"], tb["place"], tb["co"]]
    ins = [profiles.reshape(256, 128), owner_counts.reshape(1, 128), dynamics, prev_state.reshape(64, 128)]
    ins += [jnp.asarray(c) for c in consts]
    V = pltpu.VMEM
    out = pl.pallas_call(
        kernel,
        out_shape=jax.ShapeDtypeStruct((64, 128), F32),
        in_specs=[pl.BlockSpec(memory_space=pltpu.SMEM)] + [pl.BlockSpec(memory_space=pl.ANY)] * len(ins),
        out_specs=pl.BlockSpec(memory_space=V),
        scratch_shapes=[V(i.shape, i.dtype) for i in ins] + [
            *[V((128, 256), F32)] * 4, *[V((128, 128), F32)] * 2, V((8, 128), F32), V((4, 8, 128), F32),
            V((127, 1, 256), F32), V((4, 128, 128), F32), V((3, 128, 128), F32), V((64, 128), F32), V((320, 128), BF),
            pltpu.SemaphoreType.DMA((len(ins),)), pltpu.SemaphoreType.DMA((8,))],
        compiler_params=pltpu.CompilerParams(collective_id=0, has_side_effects=True),
    )(band_edges, *ins)
    return out.reshape(64, 1, 128)


def solution(mesh):
    return jax.shard_map(
        body,
        mesh=mesh,
        in_specs=(P("scans", "bins"), P(), P(), P(), P("bins", "scans", None)),
        out_specs=P("bins", "scans", None),
        check_vma=False,
    )
```

```python
import functools

import jax
import jax.numpy as jnp
import ml_dtypes
import numpy as np
from jax import lax
from jax.experimental import pallas as pl
from jax.experimental.pallas import tpu as pltpu
from jax.sharding import PartitionSpec as P

MESH = pl.DeviceIdType.MESH
BF=jnp.bfloat16; F32=jnp.float32
ND=128; NB=1<<22; M=1<<15; EPS=1e-5; NCLASS=5

def pair(a):
    a=np.asarray(a,np.float64)
    hi=a.astype(np.float32).astype(ml_dtypes.bfloat16)
    lo=(a-hi.astype(np.float64)).astype(np.float32).astype(ml_dtypes.bfloat16)
    return hi,lo
def split(x):
    hi=x.astype(BF); lo=(x-hi.astype(F32)).astype(BF)
    return hi,lo
def dot(a,b): return lax.dot_general(a,b,(((1,),(0,)),((),())),preferred_element_type=F32)
def dot_nt(a,b): return lax.dot_general(a,b,(((1,),(1,)),((),())),preferred_element_type=F32)
def dot3(a,b,d=dot):
    return d(a[0],b[0])+(d(a[0],b[1])+d(a[1],b[0]))
def tables():
    i=np.arange(128)[:,None]; j=np.arange(128)[None,:]; a=np.arange(256)[None,:]
    ang=2*np.pi*(i*j%128)/128; C,S=np.cos(ang),np.sin(ang)
    F1=np.concatenate([C,-S],0)
    MM=np.block([[C,S],[-S,C]])
    ang=2*np.pi*(i*a%256)/256; C2,S2=np.cos(ang),np.sin(ang)
    W2=np.block([[C2,S2],[-S2,C2]])
    ang=2*np.pi*(i*a)/M
    tw=np.stack([np.cos(ang),-np.sin(ang)]).astype(np.float32)
    b=np.arange(128)
    G=np.zeros((128,128))
    G[b,b//8]=1
    for m in range(16):
        g=15-m
        for bb in range(8*g+1,min(8*g+9,128)): G[bb,16+m]=1
    place=np.zeros((5,128,256))
    for q in range(5):
        for m in range(16):
            if q<4:
                place[q,m,16*q+m]=1; place[q,64+m,64+16*q+m]=1
                place[q,16+m,48-16*q+m]=1; place[q,80+m,64+48-16*q+m]=-1
        if q<4:
            place[q,40,128]=1; place[q,41,128]=1
        if q>=1:
            place[q,42,128]=1; place[q,32,64-16*q]=1; place[q,96,128-16*q]=-1
    place=place.reshape(640,256)
    co=np.zeros((5,128,128))
    for be in range(5):
        for k in range(64):
            co[be,k,k>>be]=1; co[be,64+k,64+(k>>be)]=1
    co=co.reshape(640,128)
    return dict(F1=pair(F1),MM=pair(MM),W2=pair(W2),tw=tw,G=G.astype(ml_dtypes.bfloat16),place=place.astype(ml_dtypes.bfloat16),co=co.astype(ml_dtypes.bfloat16))

def iota(shape,d): return lax.broadcasted_iota(jnp.int32,shape,d)

def stage1(R1, F1, W2, tw):
    A=dot3(F1, split(R1))
    Ar,Ai=A[:128],A[128:]
    tr,ti=tw[0],tw[1]
    Br=Ar*tr-Ai*ti; Bi=Ar*ti+Ai*tr
    B=jnp.concatenate([Br,Bi],1)
    Y=dot3(W2, split(B), dot_nt)
    Yr,Yi=Y[:128],Y[128:]
    lane=iota((1,256),1)
    nyq=jnp.sum(jnp.where(lane%2==0,Br[0:1],-Br[0:1]),axis=1,keepdims=True)
    first=(iota((128,128),0)==0)&(iota((128,128),1)==0)
    Yi=jnp.where(first,nyq,Yi)
    return jnp.concatenate([Yr,Yi],1)

def twiddle(me):
    n=iota((128,128),0); b=iota((128,128),1)
    th=(n*(128*me+b)).astype(F32)*(2*np.pi/NB)
    nn=n.astype(F32)*(2*np.pi/256)
    zero=me==0
    return jnp.cos(th),jnp.sin(th),jnp.cos(nn),jnp.sin(nn)

def stage2(R2, me, T, MM, G):
    Tr,Ts,Nr,Ns=T
    Rr,Ri=R2[:,:128],R2[:,128:]
    lane0=iota((128,128),1)==0
    zero=me==0
    Ri0=jnp.where(lane0&zero,0.0,Ri)
    Yr=Rr*Tr+Ri0*Ts; Yi=Ri0*Tr-Rr*Ts
    Er=jnp.where(zero,Ri*Nr,Yr); Ei=jnp.where(zero,-Ri*Ns,Yi)
    Y=jnp.concatenate([Yr,Yi],0); E=jnp.concatenate([Er,Ei],0)
    yh,yl=split(Y)
    Z=dot(yh,G)+dot(yl,G)
    Z=jnp.where(iota((256,128),1)==32,E[:,0:1],Z)
    zh,zl=split(Z)
    X=dot3(MM,(jnp.concatenate([yh,zh],1),jnp.concatenate([yl,zl],1)))
    Xr,Xi=X[:128,:128],X[128:,:128]; Fr,Fi=X[:128,128:],X[128:,128:]
    rows=iota((128,128),0)
    Pw=Xr*Xr+Xi*Xi
    Pw=jnp.where(lane0&(rows>=64),0.0,Pw)
    ps=jnp.sum(Pw,axis=1,keepdims=True)
    Pe=(Fr*Fr+Fi*Fi)
    lane=iota((128,128),1)
    Q=jnp.where(lane==0,ps,jnp.where(lane==32,Pe,0.0))
    Qt=jnp.transpose(Q)
    return Fr,Fi,Qt

def starts_of(counts_row):
    o=iota((128,128),0); k=iota((128,128),1)
    return jnp.sum(jnp.where(k<o,counts_row.astype(F32),0.0),axis=1,keepdims=True).astype(jnp.int32)

def onehots(starts, me):
    q4=me//4
    k=iota((128,128),1)
    def row(cl):
        return (starts+((cl-starts)&63))>>6
    main=row(q4); mir=127-row(63-q4); ext=127-row(63-((me+127)%128)//4)
    Sm=(k==main)&(k<64); Sx=(k==mir)&(k>=64); Se=(k==ext)&(k>=64)
    return Sm,Sx,Se

def stage3(Fr,Fi,S):
    Sm,Sx,Se=S
    rows=iota((128,128),0); lane=iota((128,128),1)
    keep=((rows<64)&(lane<16))|((rows>=64)&(lane>=16)&(lane<32))
    keepe=(rows>=64)&(lane==32)
    Wm=jnp.concatenate([jnp.where(keep,Fr,0.0),jnp.where(keep,Fi,0.0)],1)
    We=jnp.concatenate([jnp.where(keepe,Fr,0.0),jnp.where(keepe,Fi,0.0)],1)
    W=jnp.concatenate([Wm,We],0)
    SS=jnp.concatenate([(Sm|Sx).astype(F32).astype(BF),Se.astype(F32).astype(BF)],1)
    h,l=split(W)
    Ms=dot(SS,h)+dot(SS,l)
    return Ms[:,:128], Ms[:,128:]

def stage3b(mr,mi_rolled,S,tot):
    Sm,Sx,Se=S
    p0=tot[0:1]; p1=tot[1:2]
    z=0.0
    a=jnp.sum(jnp.where(Sm,p0,z),axis=1,keepdims=True)
    b=jnp.sum(jnp.where(Sx,p0,z),axis=1,keepdims=True)
    c=jnp.sum(jnp.where(Se,p1,z),axis=1,keepdims=True)
    lane=iota((128,128),1)
    return jnp.where(lane<40,mr,jnp.where(lane>=64,mi_rolled,jnp.where(lane==40,a,jnp.where(lane==41,b,jnp.where(lane==42,c,0.0)))))

def slot_info(counts_row, edges, me):
    k=iota((64,128),1)
    st=jnp.sum(jnp.where(k<me,counts_row.astype(F32),0.0),axis=1,keepdims=True).astype(jnp.int32)
    cn=jnp.sum(jnp.where(k==me,counts_row.astype(F32),0.0),axis=1,keepdims=True).astype(jnp.int32)
    s=iota((64,1),0)
    t=st+s
    band=sum([(t>=edges[e]).astype(jnp.int32) for e in range(1,5)])
    return t,band,s<cn

def owner_select(t):
    c=t&63; main=c<32
    j=iota((64,128),1)
    r4=4*jnp.where(main,c,63-c)
    sel=[(j==r4+q).astype(F32).astype(BF) for q in range(4)]
    sel.append((j==((4*(64-c))&127)).astype(F32).astype(BF))
    return jnp.concatenate(sel,0)

def state_part(prev, dyn, t, band):
    pr=jnp.concatenate([prev[:,:64],prev[:,64:]],0)
    band2=jnp.concatenate([band,band],0)
    cnt=64>>band2
    lane=iota((128,64),1)
    pr=jnp.where(lane<cnt,pr,0.0)
    out=jnp.zeros((128,64),F32)
    for be in range(NCLASS):
        x=jnp.where(band2==be,pr,0.0)
        out=out+dot3(split(x),split(dyn[be]),dot_nt)
    out=jnp.where(lane<cnt,out,0.0)
    return jnp.concatenate([out[:64],out[64:]],1)

def stage4(R3, sel, t, band, occ, place, co, spart):
    h,l=split(R3)
    main=(t&63)<32
    lane=iota((64,128),1)
    inmain=(lane<16)|((lane>=64)&(lane<80))|(lane==40)
    inmir=((lane>=16)&(lane<32))|((lane>=80)&(lane<96))|(lane==41)
    inext=(lane==32)|(lane==96)|(lane==42)
    res=None
    for v in (h,l):
        T=dot(sel,v)
        parts=[]
        for q in range(5):
            mk=(main&inmain&(q<4))|(jnp.logical_not(main)&((inmir&(q<4))|(inext&(q>=1))))
            parts.append(jnp.where(mk,T[64*q:64*q+64],0.0).astype(BF))
        o=dot(jnp.concatenate(parts,1),place)
        res=o if res is None else res+o
    fine=res[:,:128]; pw=res[:,128:129]
    fh,fl=split(fine)
    meas=None
    for v in (fh,fl):
        x=jnp.concatenate([jnp.where(band==be,v.astype(F32),0.0).astype(BF) for be in range(5)],1)
        o=dot(x,co)
        meas=o if meas is None else meas+o
    mp=pw/(4*512)
    scale=1.0/jnp.sqrt((8<<band).astype(F32)*(mp+EPS))
    st=iota((64,128),1)&63
    meas=jnp.where(st<(64>>band),meas*scale,0.0)
    return jnp.where(occ,meas+spart,0.0)


def kernel(x_h, cnt_h, edges_h, dyn_h, prev_h, f1h_h, f1l_h, mmh_h, mml_h, w2h_h, w2l_h, tw_h, g_h, pl_h, co_h,
           o_ref,
           x_v, cnt_v, edges_v, dyn_v, prev_v, f1h_v, f1l_v, mmh_v, mml_v, w2h_v, w2l_v, tw_v, g_v, pl_v, co_v,
           s1, r1, s2, r2, s3, r3, xs, xr, dummy, t_v, oh_v, sp_v, sel_v, csem, sem):
    me = lax.axis_index("bins")
    mx = lax.axis_index("scans")
    hs = [x_h, cnt_h, edges_h, dyn_h, prev_h, f1h_h, f1l_h, mmh_h, mml_h, w2h_h, w2l_h, tw_h, g_h, pl_h, co_h]
    vs = [x_v, cnt_v, edges_v, dyn_v, prev_v, f1h_v, f1l_v, mmh_v, mml_v, w2h_v, w2l_v, tw_v, g_v, pl_v, co_v]
    loads = [pltpu.make_async_copy(h, v, csem.at[i]) for i, (h, v) in enumerate(zip(hs, vs))]
    loads[0].start()
    bar = pltpu.get_barrier_semaphore()

    z16, y2, c1 = me & 112, me & 14, me & 1
    ys = [((y2 + 2 * d) & 14) | (c1 ^ c) for d in (4, 3, 5, 2, 6, 1, 7, 0) for c in (1, 0)]

    def far_first(act):
        def ring(i, c):
            d = 4 + jnp.where((i & 1) == 1, -((i + 1) >> 1), i >> 1)
            zz = (z16 + 16 * d) & 112
            for y in ys:
                act(zz | y)
            return c
        lax.fori_loop(0, 7, ring, 0)
        for y in ys[:-1]:
            act(z16 | y)

    far_first(lambda j: pl.semaphore_signal(bar, inc=1, device_id={"bins": j}, device_id_type=MESH))
    for i in range(1, 4):
        pl.semaphore_signal(bar, inc=1, device_id={"scans": lax.rem(mx + i, 4)}, device_id_type=MESH)
    for ld in loads[1:]:
        ld.start()
    loads[0].wait()
    s1[...] = jnp.concatenate([jnp.transpose(x_v[0:128, :]), jnp.transpose(x_v[128:256, :])], 1)
    pl.semaphore_wait(bar, ND + 2)

    def send_all(s, r, k):
        def one(j):
            pltpu.make_async_remote_copy(s.at[pl.ds(j, 1)], r.at[pl.ds(me, 1)], sem.at[k], sem.at[k + 1],
                                         device_id={"bins": j}, device_id_type=MESH).start()
        far_first(one)

    def wait_all(w, k):
        d = dummy.at[:, :, pl.ds(0, w)]
        pltpu.make_async_copy(d, d, sem.at[k]).wait()

    send_all(s1, r1, 0)
    r1[pl.ds(me, 1), :] = s1[pl.ds(me, 1), :]
    for ld in loads[1:]:
        ld.wait()
    T = twiddle(me)
    for i in range(4):
        t_v[i] = T[i]
    counts = cnt_v[...]
    for i, m in enumerate(onehots(starts_of(counts), me)):
        oh_v[i] = m.astype(F32)
    edges = [edges_v[i] for i in range(6)]
    t, band, occ = slot_info(counts, edges, me)
    sp_v[...] = state_part(prev_v[...], dyn_v, t, band)
    sel_v[...] = owner_select(t)
    wait_all(256, 1)
    wait_all(256, 0)

    s2[...] = stage1(r1[...], (f1h_v[...], f1l_v[...]), (w2h_v[...], w2l_v[...]), tw_v)
    send_all(s2, r2, 2)
    r2[pl.ds(me, 1), :] = s2[pl.ds(me, 1), :]
    wait_all(256, 3)
    wait_all(256, 2)

    Fr, Fi, Qt = stage2(r2[...], me, [t_v[i] for i in range(4)], (mmh_v[...], mml_v[...]), g_v[...])
    xs[...] = Qt[0:8]
    xs[1:2, :] = Qt[32:33]
    for i in range(1, 4):
        pltpu.make_async_remote_copy(xs, xr.at[mx], sem.at[4], sem.at[5],
                                     device_id={"scans": lax.rem(mx + i, 4)}, device_id_type=MESH).start()
    xr[mx] = xs[...]
    S = [oh_v[i] > 0.5 for i in range(3)]
    mr, mi = stage3(Fr, Fi, S)
    mi = pltpu.roll(mi, 64, 1)
    d = xr.at[pl.ds(0, 3)]
    pltpu.make_async_copy(d, d, sem.at[5]).wait()
    pltpu.make_async_copy(d, d, sem.at[4]).wait()
    tot = xr[0] + xr[1] + xr[2] + xr[3]
    s3[...] = stage3b(mr, mi, S, tot)
    send_all(s3, r3, 6)
    r3[pl.ds(me, 1), :] = s3[pl.ds(me, 1), :]
    wait_all(128, 7)
    wait_all(128, 6)
    t, band, occ = slot_info(cnt_v[...], edges, me)
    o_ref[...] = stage4(r3[...], sel_v[...], t, band, occ, pl_v[...], co_v[...], sp_v[...])


def emit(a_ref, o_ref, sem):
    c = pltpu.make_async_copy(a_ref, o_ref, sem)
    c.start()
    c.wait()


def body(profiles, band_edges, owner_counts, dynamics, prev_state):
    tb = tables()
    consts = [*tb["F1"], *tb["MM"], *tb["W2"], tb["tw"], tb["G"], tb["place"], tb["co"]]
    ins = [profiles.reshape(256, 128), owner_counts.reshape(1, 128), band_edges, dynamics, prev_state.reshape(64, 128)]
    ins += [jnp.asarray(c) for c in consts]
    V = pltpu.VMEM
    out = pl.pallas_call(
        kernel,
        out_shape=V((64, 128), F32),
        in_specs=[pl.BlockSpec(memory_space=pltpu.HBM)] * len(ins),
        out_specs=pl.BlockSpec(memory_space=V),
        scratch_shapes=[(pltpu.SMEM if i.shape == (6,) else V)(i.shape, i.dtype) for i in ins] + [
            *[V((128, 256), F32)] * 4, *[V((128, 128), F32)] * 2, V((8, 128), F32), V((4, 8, 128), F32),
            V((127, 1, 256), F32), V((4, 128, 128), F32), V((3, 128, 128), F32), V((64, 128), F32), V((320, 128), BF),
            pltpu.SemaphoreType.DMA((len(ins),)), pltpu.SemaphoreType.DMA((8,))],
        compiler_params=pltpu.CompilerParams(collective_id=0, has_side_effects=True, vmem_limit_bytes=48 << 20),
    )(*[pltpu.with_memory_space_constraint(i, pltpu.HBM) for i in ins])
    return out.reshape(64, 1, 128)


def solution(mesh):
    return jax.shard_map(
        body,
        mesh=mesh,
        in_specs=(P("scans", "bins"), P(), P(), P(), P("bins", "scans", None)),
        out_specs=P("bins", "scans", None),
        check_vma=False,
    )
```

```python
import functools

import jax
import jax.numpy as jnp
import ml_dtypes
import numpy as np
from jax import lax
from jax.experimental import pallas as pl
from jax.experimental.pallas import tpu as pltpu
from jax.sharding import PartitionSpec as P

MESH = pl.DeviceIdType.MESH
BF=jnp.bfloat16; F32=jnp.float32
ND=128; NB=1<<22; M=1<<15; EPS=1e-5; NCLASS=5

def pair(a):
    a=np.asarray(a,np.float64)
    hi=a.astype(np.float32).astype(ml_dtypes.bfloat16)
    lo=(a-hi.astype(np.float64)).astype(np.float32).astype(ml_dtypes.bfloat16)
    return hi,lo
def split(x):
    hi=x.astype(BF); lo=(x-hi.astype(F32)).astype(BF)
    return hi,lo
def dot(a,b): return lax.dot_general(a,b,(((1,),(0,)),((),())),preferred_element_type=F32)
def dot_nt(a,b): return lax.dot_general(a,b,(((1,),(1,)),((),())),preferred_element_type=F32)
def dot3(a,b,d=dot):
    return d(a[0],b[0])+(d(a[0],b[1])+d(a[1],b[0]))
def tables():
    i=np.arange(128)[:,None]; j=np.arange(128)[None,:]; a=np.arange(256)[None,:]
    ang=2*np.pi*(i*j%128)/128; C,S=np.cos(ang),np.sin(ang)
    F1=np.concatenate([C,-S],0)
    MM=np.block([[C,S],[-S,C]])
    ang=2*np.pi*(i*a%256)/256; C2,S2=np.cos(ang),np.sin(ang)
    W2=np.block([[C2,S2]])
    ang=2*np.pi*(i*a)/M
    tw=np.stack([np.cos(ang),-np.sin(ang)]).astype(np.float32)
    b=np.arange(128)
    G=np.zeros((128,128))
    G[b,b//8]=1
    for m in range(16):
        g=15-m
        for bb in range(8*g+1,min(8*g+9,128)): G[bb,16+m]=1
    place=np.zeros((5,128,256))
    for q in range(5):
        for m in range(16):
            if q<4:
                place[q,m,16*q+m]=1; place[q,64+m,64+16*q+m]=1
                place[q,16+m,48-16*q+m]=1; place[q,80+m,64+48-16*q+m]=-1
        if q<4:
            place[q,40,128]=1; place[q,41,128]=1
        if q>=1:
            place[q,42,128]=1; place[q,32,64-16*q]=1; place[q,96,128-16*q]=-1
    place=place.reshape(640,256)
    co=np.zeros((5,128,128))
    for be in range(5):
        for k in range(64):
            co[be,k,k>>be]=1; co[be,64+k,64+(k>>be)]=1
    co=co.reshape(640,128)
    f1h,f1l=pair(F1)
    return dict(F1=(np.concatenate([f1h,f1h],1),f1l),MM=pair(MM),W2=pair(W2),tw=tw,G=np.concatenate([G,G],0).astype(ml_dtypes.bfloat16),place=place.astype(ml_dtypes.bfloat16),co=co.astype(ml_dtypes.bfloat16))

def iota(shape,d): return lax.broadcasted_iota(jnp.int32,shape,d)

def stage1(R1, F1, W2, tw):
    gh,gl=split(R1)
    A=dot(F1[0],jnp.concatenate([gh,gl],0))+dot(F1[1],gh)
    Ar,Ai=A[:128],A[128:]
    tr,ti=tw[0],tw[1]
    Br=Ar*tr-Ai*ti; Bi=Ar*ti+Ai*tr
    (rh,rl),(ih,il)=split(Br),split(Bi)
    def both(r,i):
        return jnp.concatenate([jnp.concatenate([r,i],1),jnp.concatenate([i,-r],1)],0)
    Y=dot3(W2, (both(rh,ih),both(rl,il)), dot_nt)
    lane=iota((1,256),1)
    nyq=jnp.sum(jnp.where(lane%2==0,Br[0:1],-Br[0:1]),axis=1,keepdims=True)
    first=(iota((128,256),0)==0)&(iota((128,256),1)==128)
    Y=jnp.where(first,nyq,Y)
    return Y[:,:128],Y[:,128:]

def twiddle(me):
    n=iota((128,128),0); b=iota((128,128),1)
    th=(n*(128*me+b)).astype(F32)*(2*np.pi/NB)
    nn=n.astype(F32)*(2*np.pi/256)
    zero=me==0
    return jnp.cos(th),jnp.sin(th),jnp.cos(nn),jnp.sin(nn)

def stage2(R2, me, T, MM):
    Tr,Ts,Nr,Ns=T
    Rr,Ri=R2[:,:128],R2[:,128:]
    lane0=iota((128,128),1)==0
    zero=me==0
    Ri0=jnp.where(lane0&zero,0.0,Ri)
    Yr=Rr*Tr+Ri0*Ts; Yi=Ri0*Tr-Rr*Ts
    Er=jnp.where(zero,Ri*Nr,Yr); Ei=jnp.where(zero,-Ri*Ns,Yi)
    Y=jnp.concatenate([Yr,Yi],0); E=jnp.concatenate([Er,Ei],0)
    yh,yl=split(Y); eh,el=split(E)
    X=dot3(MM,(jnp.concatenate([yh,eh],1),jnp.concatenate([yl,el],1)))
    Xr,Xi,Er,Ei=X[:128,:128],X[128:,:128],X[:128,128:],X[128:,128:]
    rows=iota((128,128),0)
    Pw=jnp.where(lane0&(rows>=64),0.0,Xr*Xr+Xi*Xi)
    Pe=jnp.where(lane0,Er*Er+Ei*Ei,0.0)
    ph,pl_=split(jnp.concatenate([Pw,Pe],0))
    sums=dot_nt(jnp.ones((8,256),BF),jnp.concatenate([ph,pl_],1))
    return sums,(yh,yl),(Er,Ei)

def stage2b(y, E, MM, G):
    Z=dot(jnp.concatenate(y,1),G)
    F=dot3(MM,split(Z))
    return F[:128],F[128:]

def starts_of(counts_row):
    o=iota((128,128),0); k=iota((128,128),1)
    return jnp.sum(jnp.where(k<o,counts_row.astype(F32),0.0),axis=1,keepdims=True).astype(jnp.int32)

def onehots(starts, me):
    q4=me//4
    k=iota((128,128),1)
    def row(cl):
        return (starts+((cl-starts)&63))>>6
    main=row(q4); mir=127-row(63-q4); ext=127-row(63-((me+127)%128)//4)
    Sm=(k==main)&(k<64); Sx=(k==mir)&(k>=64); Se=(k==ext)&(k>=64)
    return Sm,Sx,Se

def stage3(Fr,Fi,E,S):
    Sm,Sx,Se=S
    rows=iota((128,128),0); lane=iota((128,128),1)
    keep=((rows<64)&(lane<16))|((rows>=64)&(lane>=16)&(lane<32))
    keepe=(rows>=64)&(lane==32)
    Wm=jnp.concatenate([jnp.where(keep,Fr,0.0),jnp.where(keep,Fi,0.0)],1)
    We=jnp.concatenate([jnp.where(keepe,E[0][:,0:1],0.0),jnp.where(keepe,E[1][:,0:1],0.0)],1)
    W=jnp.concatenate([Wm,We],0)
    SS=jnp.concatenate([(Sm|Sx).astype(F32).astype(BF),Se.astype(F32).astype(BF)],1)
    h,l=split(W)
    Ms=dot(SS,h)+dot(SS,l)
    return Ms[:,:128], Ms[:,128:]

def stage3b(mr,mi_rolled,S,tot):
    Sm,Sx,Se=S
    p0=tot[0:1]; p1=tot[4:5]
    z=0.0
    a=jnp.sum(jnp.where(Sm,p0,z),axis=1,keepdims=True)
    b=jnp.sum(jnp.where(Sx,p0,z),axis=1,keepdims=True)
    c=jnp.sum(jnp.where(Se,p1,z),axis=1,keepdims=True)
    lane=iota((128,128),1)
    return jnp.where(lane<40,mr,jnp.where(lane>=64,mi_rolled,jnp.where(lane==40,a,jnp.where(lane==41,b,jnp.where(lane==42,c,0.0)))))

def slot_info(counts_row, edges, me):
    k=iota((64,128),1)
    st=jnp.sum(jnp.where(k<me,counts_row.astype(F32),0.0),axis=1,keepdims=True).astype(jnp.int32)
    cn=jnp.sum(jnp.where(k==me,counts_row.astype(F32),0.0),axis=1,keepdims=True).astype(jnp.int32)
    s=iota((64,1),0)
    t=st+s
    band=sum([(t>=edges[e]).astype(jnp.int32) for e in range(1,5)])
    return t,band,s<cn

def owner_select(t):
    c=t&63; main=c<32
    j=iota((64,128),1)
    r4=4*jnp.where(main,c,63-c)
    sel=[(j==r4+q).astype(F32).astype(BF) for q in range(4)]
    sel.append((j==((4*(64-c))&127)).astype(F32).astype(BF))
    return jnp.concatenate(sel,0)

def state_part(prev, dyn, t, band):
    pr=jnp.concatenate([prev[:,:64],prev[:,64:]],0)
    band2=jnp.concatenate([band,band],0)
    cnt=64>>band2
    lane=iota((128,64),1)
    pr=jnp.where(lane<cnt,pr,0.0)
    out=jnp.zeros((128,64),F32)
    for be in range(NCLASS):
        x=jnp.where(band2==be,pr,0.0)
        out=out+dot3(split(x),split(dyn[be]),dot_nt)
    out=jnp.where(lane<cnt,out,0.0)
    return jnp.concatenate([out[:64],out[64:]],1)

def stage4(R3, sel, t, band, occ, place, co, spart):
    h,l=split(R3)
    main=(t&63)<32
    lane=iota((64,128),1)
    inmain=(lane<16)|((lane>=64)&(lane<80))|(lane==40)
    inmir=((lane>=16)&(lane<32))|((lane>=80)&(lane<96))|(lane==41)
    inext=(lane==32)|(lane==96)|(lane==42)
    T=dot(sel,jnp.concatenate([h,l],1))
    halves=[]
    for v in (T[:,:128],T[:,128:]):
        parts=[]
        for q in range(5):
            mk=(main&inmain&(q<4))|(jnp.logical_not(main)&((inmir&(q<4))|(inext&(q>=1))))
            parts.append(jnp.where(mk,v[64*q:64*q+64],0.0).astype(BF))
        halves.append(jnp.concatenate(parts,1))
    res=dot(jnp.concatenate(halves,0),place)
    res=res[:64]+res[64:]
    fine=res[:,:128]; pw=res[:,128:129]
    fhl=jnp.concatenate(split(fine),0).astype(F32)
    band2=jnp.concatenate([band,band],0)
    x=jnp.concatenate([jnp.where(band2==be,fhl,0.0).astype(BF) for be in range(5)],1)
    meas=dot(x,co)
    meas=meas[:64]+meas[64:]
    mp=pw/(4*512)
    scale=1.0/jnp.sqrt((8<<band).astype(F32)*(mp+EPS))
    st=iota((64,128),1)&63
    meas=jnp.where(st<(64>>band),meas*scale,0.0)
    return jnp.where(occ,meas+spart,0.0)


EVEN, ODD = pl.ds(0, 128, stride=2), pl.ds(1, 128, stride=2)


def rows_of(j, n):
    return pl.ds(pl.multiple_of(n * j, n), n)


def kernel(x_h, cnt_h, edges_h, dyn_h, prev_h, f1h_h, f1l_h, mmh_h, mml_h, w2h_h, w2l_h, tw_h, g_h, pl_h, co_h,
           o_ref,
           x_v, cnt_v, edges_v, dyn_v, prev_v, f1h_v, f1l_v, mmh_v, mml_v, w2h_v, w2l_v, tw_v, g_v, pl_v, co_v,
           s1, r1, s2, r2, s3, r3, xs, xr, dummy, t_v, oh_v, sp_v, sel_v, csem, sem):
    me = lax.axis_index("bins")
    mx = lax.axis_index("scans")
    hs = [x_h, cnt_h, edges_h, dyn_h, prev_h, f1h_h, f1l_h, mmh_h, mml_h, w2h_h, w2l_h, tw_h, g_h, pl_h, co_h]
    vs = [x_v, cnt_v, edges_v, dyn_v, prev_v, f1h_v, f1l_v, mmh_v, mml_v, w2h_v, w2l_v, tw_v, g_v, pl_v, co_v]
    loads = [pltpu.make_async_copy(h, v, csem.at[i]) for i, (h, v) in enumerate(zip(hs, vs))]
    loads[0].start()
    bar = pltpu.get_barrier_semaphore()

    z16, y2, c1 = me & 112, me & 14, me & 1
    ys = [((y2 + 2 * d) & 14) | (c1 ^ c) for d in (4, 5, 3, 6, 2, 7, 1, 0) for c in (1, 0)]

    def far_first(act):
        def ring(i, c):
            d = 4 + jnp.where((i & 1) == 1, -((i + 1) >> 1), i >> 1)
            zz = (z16 + 16 * d) & 112
            for y in ys:
                act(zz | y)
            return c
        lax.fori_loop(0, 7, ring, 0)
        for y in ys[:-1]:
            act(z16 | y)

    far_first(lambda j: pl.semaphore_signal(bar, inc=1, device_id={"bins": j}, device_id_type=MESH))
    for i in range(1, 4):
        pl.semaphore_signal(bar, inc=1, device_id={"scans": lax.rem(mx + i, 4)}, device_id_type=MESH)
    for ld in loads[1:]:
        ld.start()
    loads[0].wait()
    s1[EVEN, :] = jnp.transpose(x_v[0:128, :])
    s1[ODD, :] = jnp.transpose(x_v[128:256, :])
    pl.semaphore_wait(bar, ND + 2)

    def send_all(s, r, k, n=2):
        def one(j):
            pltpu.make_async_remote_copy(s.at[rows_of(j, n)], r.at[rows_of(me, n)], sem.at[k], sem.at[k + 1],
                                         device_id={"bins": j}, device_id_type=MESH).start()
        far_first(one)

    def wait_all(w, k):
        d = dummy.at[:, :, pl.ds(0, w)]
        pltpu.make_async_copy(d, d, sem.at[k]).wait()

    send_all(s1, r1, 0)
    r1[rows_of(me, 2), :] = s1[rows_of(me, 2), :]
    for ld in loads[1:]:
        ld.wait()
    T = twiddle(me)
    for i in range(4):
        t_v[i] = T[i]
    counts = cnt_v[...]
    for i, m in enumerate(onehots(starts_of(counts), me)):
        oh_v[i] = m.astype(F32)
    edges = [edges_v[i] for i in range(6)]
    t, band, occ = slot_info(counts, edges, me)
    sp_v[...] = state_part(prev_v[...], dyn_v, t, band)
    sel_v[...] = owner_select(t)
    wait_all(256, 1)
    wait_all(256, 0)

    s2[EVEN, :], s2[ODD, :] = stage1(jnp.concatenate([r1[EVEN, :], r1[ODD, :]], 1), (f1h_v[...], f1l_v[...]), (w2h_v[...], w2l_v[...]), tw_v)
    send_all(s2, r2, 2)
    r2[rows_of(me, 2), :] = s2[rows_of(me, 2), :]
    wait_all(256, 3)
    wait_all(256, 2)

    sums, y, E = stage2(jnp.concatenate([r2[EVEN, :], r2[ODD, :]], 1), me, [t_v[i] for i in range(4)], (mmh_v[...], mml_v[...]))
    xs[0:4, :] = sums[0:4, 0:128]
    xs[4:8, :] = sums[4:8, 128:256]
    for i in range(1, 4):
        pltpu.make_async_remote_copy(xs, xr.at[mx], sem.at[4], sem.at[5],
                                     device_id={"scans": lax.rem(mx + i, 4)}, device_id_type=MESH).start()
    xr[mx] = xs[...]
    S = [oh_v[i] > 0.5 for i in range(3)]
    Fr, Fi = stage2b(y, E, (mmh_v[...], mml_v[...]), g_v[...])
    mr, mi = stage3(Fr, Fi, E, S)
    mi = pltpu.roll(mi, 64, 1)
    d = xr.at[pl.ds(0, 3)]
    pltpu.make_async_copy(d, d, sem.at[5]).wait()
    pltpu.make_async_copy(d, d, sem.at[4]).wait()
    tot = xr[0] + xr[1] + xr[2] + xr[3]
    s3[...] = stage3b(mr, mi, S, tot)
    send_all(s3, r3, 6, 1)
    r3[pl.ds(me, 1), :] = s3[pl.ds(me, 1), :]
    wait_all(128, 7)
    wait_all(128, 6)
    t, band, occ = slot_info(cnt_v[...], edges, me)
    o_ref[...] = stage4(r3[...], sel_v[...], t, band, occ, pl_v[...], co_v[...], sp_v[...])


def emit(a_ref, o_ref, sem):
    c = pltpu.make_async_copy(a_ref, o_ref, sem)
    c.start()
    c.wait()


def body(profiles, band_edges, owner_counts, dynamics, prev_state):
    tb = tables()
    consts = [*tb["F1"], *tb["MM"], *tb["W2"], tb["tw"], tb["G"], tb["place"], tb["co"]]
    ins = [profiles.reshape(256, 128), owner_counts.reshape(1, 128), band_edges, dynamics, prev_state.reshape(64, 128)]
    ins += [jnp.asarray(c) for c in consts]
    V = pltpu.VMEM
    out = pl.pallas_call(
        kernel,
        out_shape=V((64, 128), F32),
        in_specs=[pl.BlockSpec(memory_space=pltpu.HBM)] * len(ins),
        out_specs=pl.BlockSpec(memory_space=V),
        scratch_shapes=[(pltpu.SMEM if i.shape == (6,) else V)(i.shape, i.dtype) for i in ins] + [
            *[V((256, 128), F32)] * 4, *[V((128, 128), F32)] * 2, V((8, 128), F32), V((4, 8, 128), F32),
            V((127, 1, 256), F32), V((4, 128, 128), F32), V((3, 128, 128), F32), V((64, 128), F32), V((320, 128), BF),
            pltpu.SemaphoreType.DMA((len(ins),)), pltpu.SemaphoreType.DMA((8,))],
        compiler_params=pltpu.CompilerParams(collective_id=0, has_side_effects=True, vmem_limit_bytes=48 << 20),
    )(*[pltpu.with_memory_space_constraint(i, pltpu.HBM) for i in ins])
    return out.reshape(64, 1, 128)


def solution(mesh):
    return jax.shard_map(
        body,
        mesh=mesh,
        in_specs=(P("scans", "bins"), P(), P(), P(), P("bins", "scans", None)),
        out_specs=P("bins", "scans", None),
        check_vma=False,
    )
```

```python
import functools

import jax
import jax.numpy as jnp
import ml_dtypes
import numpy as np
from jax import lax
from jax.experimental import pallas as pl
from jax.experimental.pallas import tpu as pltpu
from jax.sharding import PartitionSpec as P

MESH = pl.DeviceIdType.MESH
BF=jnp.bfloat16; F32=jnp.float32
ND=128; NB=1<<22; M=1<<15; EPS=1e-5; NCLASS=5

def triple(a):
    parts=[]
    for _ in range(3):
        parts.append(a.astype(np.float32).astype(ml_dtypes.bfloat16))
        a=a-parts[-1].astype(np.float64)
    return parts
def split(x):
    hi=x.astype(BF); lo=(x-hi.astype(F32)).astype(BF)
    return hi,lo
def dot(a,b): return lax.dot_general(a,b,(((1,),(0,)),((),())),preferred_element_type=F32)
def split3(x):
    p=x.astype(BF); r=x-p.astype(F32); q=r.astype(BF)
    return p,q,(r-q.astype(F32)).astype(BF)
def dot6(a,b,d=None):
    d=d or dot
    return d(a[0],b[0])+((d(a[0],b[1])+d(a[1],b[0]))+((d(a[0],b[2])+d(a[2],b[0]))+d(a[1],b[1])))
def dot_nt(a,b): return lax.dot_general(a,b,(((1,),(1,)),((),())),preferred_element_type=F32)
def dot3(a,b,d=dot):
    return d(a[0],b[0])+(d(a[0],b[1])+d(a[1],b[0]))
def tables():
    i=np.arange(128)[:,None]; j=np.arange(128)[None,:]; a=np.arange(256)[None,:]
    ang=2*np.pi*(i*j%128)/128; C,S=np.cos(ang),np.sin(ang)
    F1=np.concatenate([C,-S],0)
    MM=np.block([[C,S],[-S,C]])
    ang=2*np.pi*(i*a%256)/256; C2,S2=np.cos(ang),np.sin(ang)
    W2=np.block([[C2,S2]])
    ang=2*np.pi*(i*a)/M
    tw=np.stack([np.cos(ang),-np.sin(ang)]).astype(np.float32)
    b=np.arange(128)
    G=np.zeros((128,128))
    G[b,b//8]=1
    for m in range(16):
        g=15-m
        for bb in range(8*g+1,min(8*g+9,128)): G[bb,16+m]=1
    place=np.zeros((5,128,256))
    for q in range(5):
        for m in range(16):
            if q<4:
                place[q,m,16*q+m]=1; place[q,64+m,64+16*q+m]=1
                place[q,16+m,48-16*q+m]=1; place[q,80+m,64+48-16*q+m]=-1
        if q<4:
            place[q,40,128]=1; place[q,41,128]=1
        if q>=1:
            place[q,42,128]=1; place[q,32,64-16*q]=1; place[q,96,128-16*q]=-1
    place=place.reshape(640,256)
    co=np.zeros((5,128,128))
    for be in range(5):
        for k in range(64):
            co[be,k,k>>be]=1; co[be,64+k,64+(k>>be)]=1
    co=co.reshape(640,128)
    f0,f1,f2=triple(F1)
    return dict(F1=[np.concatenate(f,1) for f in ((f0,f0),(f1,f1),(f0,f2))],MM=triple(MM),W2=triple(W2),tw=tw,G=np.concatenate([G,G],0).astype(ml_dtypes.bfloat16),place=place.astype(ml_dtypes.bfloat16),co=co.astype(ml_dtypes.bfloat16))

def iota(shape,d): return lax.broadcasted_iota(jnp.int32,shape,d)

def stage1(R1, F1, W2, tw):
    g0,g1,g2=split3(R1)
    g01=jnp.concatenate([g0,g1],0)
    A=dot(F1[0],g01)+(dot(F1[1],g01)+dot(F1[2],jnp.concatenate([g2,g0],0)))
    Ar,Ai=A[:128],A[128:]
    tr,ti=tw[0],tw[1]
    Br=Ar*tr-Ai*ti; Bi=Ar*ti+Ai*tr
    rs,qs=split3(Br),split3(Bi)
    def both(r,i):
        return jnp.concatenate([jnp.concatenate([r,i],1),jnp.concatenate([i,-r],1)],0)
    Y=dot6(W2, [both(r,i) for r,i in zip(rs,qs)], dot_nt)
    lane=iota((1,256),1)
    nyq=jnp.sum(jnp.where(lane%2==0,Br[0:1],-Br[0:1]),axis=1,keepdims=True)
    first=(iota((128,256),0)==0)&(iota((128,256),1)==128)
    Y=jnp.where(first,nyq,Y)
    return Y[:,:128],Y[:,128:]

def twiddle(me):
    n=iota((128,128),0); b=iota((128,128),1)
    th=(n*(128*me+b)).astype(F32)*(2*np.pi/NB)
    nn=n.astype(F32)*(2*np.pi/256)
    zero=me==0
    return jnp.cos(th),jnp.sin(th),jnp.cos(nn),jnp.sin(nn)

def stage2(R2, me, T, MM):
    Tr,Ts,Nr,Ns=T
    Rr,Ri=R2[:,:128],R2[:,128:]
    lane0=iota((128,128),1)==0
    zero=me==0
    Ri0=jnp.where(lane0&zero,0.0,Ri)
    Yr=Rr*Tr+Ri0*Ts; Yi=Ri0*Tr-Rr*Ts
    Er=jnp.where(zero,Ri*Nr,Yr); Ei=jnp.where(zero,-Ri*Ns,Yi)
    Y=jnp.concatenate([Yr,Yi],0); E=jnp.concatenate([Er,Ei],0)
    ys,es=split3(Y),split3(E)
    X=dot6(MM,[jnp.concatenate([y,e],1) for y,e in zip(ys,es)])
    Xr,Xi,Er,Ei=X[:128,:128],X[128:,:128],X[:128,128:],X[128:,128:]
    rows=iota((128,128),0)
    Pw=jnp.where(lane0&(rows>=64),0.0,Xr*Xr+Xi*Xi)
    Pe=jnp.where(lane0,Er*Er+Ei*Ei,0.0)
    ph,pl_=split(jnp.concatenate([Pw,Pe],0))
    sums=dot_nt(jnp.ones((8,256),BF),jnp.concatenate([ph,pl_],1))
    return sums,ys,(Er,Ei)

def stage2b(y, E, MM, G):
    Z=dot(jnp.concatenate(y[:2],1),G)+dot(y[2],G[:128])
    F=dot6(MM,split3(Z))
    return F[:128],F[128:]

def starts_of(counts_row):
    o=iota((128,128),0); k=iota((128,128),1)
    return jnp.sum(jnp.where(k<o,counts_row.astype(F32),0.0),axis=1,keepdims=True).astype(jnp.int32)

def onehots(starts, me):
    q4=me//4
    k=iota((128,128),1)
    def row(cl):
        return (starts+((cl-starts)&63))>>6
    main=row(q4); mir=127-row(63-q4); ext=127-row(63-((me+127)%128)//4)
    Sm=(k==main)&(k<64); Sx=(k==mir)&(k>=64); Se=(k==ext)&(k>=64)
    return Sm,Sx,Se

def stage3(Fr,Fi,E,S):
    Sm,Sx,Se=S
    rows=iota((128,128),0); lane=iota((128,128),1)
    keep=((rows<64)&(lane<16))|((rows>=64)&(lane>=16)&(lane<32))
    keepe=(rows>=64)&(lane==32)
    Wm=jnp.concatenate([jnp.where(keep,Fr,0.0),jnp.where(keep,Fi,0.0)],1)
    We=jnp.concatenate([jnp.where(keepe,E[0][:,0:1],0.0),jnp.where(keepe,E[1][:,0:1],0.0)],1)
    W=jnp.concatenate([Wm,We],0)
    SS=jnp.concatenate([(Sm|Sx).astype(F32).astype(BF),Se.astype(F32).astype(BF)],1)
    h,l=split(W)
    Ms=dot(SS,h)+dot(SS,l)
    return Ms[:,:128], Ms[:,128:]

def stage3b(mr,mi_rolled,S,tot):
    Sm,Sx,Se=S
    p0=tot[0:1]; p1=tot[4:5]
    z=0.0
    a=jnp.sum(jnp.where(Sm,p0,z),axis=1,keepdims=True)
    b=jnp.sum(jnp.where(Sx,p0,z),axis=1,keepdims=True)
    c=jnp.sum(jnp.where(Se,p1,z),axis=1,keepdims=True)
    lane=iota((128,128),1)
    return jnp.where(lane<40,mr,jnp.where(lane>=64,mi_rolled,jnp.where(lane==40,a,jnp.where(lane==41,b,jnp.where(lane==42,c,0.0)))))

def slot_info(counts_row, edges, me):
    k=iota((64,128),1)
    st=jnp.sum(jnp.where(k<me,counts_row.astype(F32),0.0),axis=1,keepdims=True).astype(jnp.int32)
    cn=jnp.sum(jnp.where(k==me,counts_row.astype(F32),0.0),axis=1,keepdims=True).astype(jnp.int32)
    s=iota((64,1),0)
    t=st+s
    band=sum([(t>=edges[e]).astype(jnp.int32) for e in range(1,5)])
    return t,band,s<cn

def owner_select(t):
    c=t&63; main=c<32
    j=iota((64,128),1)
    r4=4*jnp.where(main,c,63-c)
    sel=[(j==r4+q).astype(F32).astype(BF) for q in range(4)]
    sel.append((j==((4*(64-c))&127)).astype(F32).astype(BF))
    return jnp.concatenate(sel,0)

def state_part(prev, dyn, t, band):
    pr=jnp.concatenate([prev[:,:64],prev[:,64:]],0)
    band2=jnp.concatenate([band,band],0)
    cnt=64>>band2
    lane=iota((128,64),1)
    pr=jnp.where(lane<cnt,pr,0.0)
    out=jnp.zeros((128,64),F32)
    for be in range(NCLASS):
        x=jnp.where(band2==be,pr,0.0)
        out=out+dot6(split3(x),split3(dyn[be]),dot_nt)
    out=jnp.where(lane<cnt,out,0.0)
    return jnp.concatenate([out[:64],out[64:]],1)

def stage4(R3, sel, t, band, occ, place, co, spart):
    h,l=split(R3)
    main=(t&63)<32
    lane=iota((64,128),1)
    inmain=(lane<16)|((lane>=64)&(lane<80))|(lane==40)
    inmir=((lane>=16)&(lane<32))|((lane>=80)&(lane<96))|(lane==41)
    inext=(lane==32)|(lane==96)|(lane==42)
    T=dot(sel,jnp.concatenate([h,l],1))
    halves=[]
    for v in (T[:,:128],T[:,128:]):
        parts=[]
        for q in range(5):
            mk=(main&inmain&(q<4))|(jnp.logical_not(main)&((inmir&(q<4))|(inext&(q>=1))))
            parts.append(jnp.where(mk,v[64*q:64*q+64],0.0).astype(BF))
        halves.append(jnp.concatenate(parts,1))
    res=dot(jnp.concatenate(halves,0),place)
    res=res[:64]+res[64:]
    fine=res[:,:128]; pw=res[:,128:129]
    fhl=jnp.concatenate(split(fine),0).astype(F32)
    band2=jnp.concatenate([band,band],0)
    x=jnp.concatenate([jnp.where(band2==be,fhl,0.0).astype(BF) for be in range(5)],1)
    meas=dot(x,co)
    meas=meas[:64]+meas[64:]
    mp=pw/(4*512)
    scale=1.0/jnp.sqrt((8<<band).astype(F32)*(mp+EPS))
    st=iota((64,128),1)&63
    meas=jnp.where(st<(64>>band),meas*scale,0.0)
    return jnp.where(occ,meas+spart,0.0)


EVEN, ODD = pl.ds(0, 128, stride=2), pl.ds(1, 128, stride=2)


def rows_of(j, n):
    return pl.ds(pl.multiple_of(n * j, n), n)


def kernel(x_h, cnt_h, edges_h, dyn_h, prev_h, f1a_h, f1b_h, f1c_h, mma_h, mmb_h, mmc_h, w2a_h, w2b_h, w2c_h, tw_h, g_h, pl_h, co_h,
           o_ref,
           x_v, cnt_v, edges_v, dyn_v, prev_v, f1a_v, f1b_v, f1c_v, mma_v, mmb_v, mmc_v, w2a_v, w2b_v, w2c_v, tw_v, g_v, pl_v, co_v,
           s1, r1, s2, r2, s3, r3, xs, xr, dummy, t_v, oh_v, sp_v, sel_v, csem, sem):
    me = lax.axis_index("bins")
    mx = lax.axis_index("scans")
    hs = [x_h, cnt_h, edges_h, dyn_h, prev_h, f1a_h, f1b_h, f1c_h, mma_h, mmb_h, mmc_h, w2a_h, w2b_h, w2c_h, tw_h, g_h, pl_h, co_h]
    vs = [x_v, cnt_v, edges_v, dyn_v, prev_v, f1a_v, f1b_v, f1c_v, mma_v, mmb_v, mmc_v, w2a_v, w2b_v, w2c_v, tw_v, g_v, pl_v, co_v]
    loads = [pltpu.make_async_copy(h, v, csem.at[i]) for i, (h, v) in enumerate(zip(hs, vs))]
    loads[0].start()
    bar = pltpu.get_barrier_semaphore()

    z16, y2, c1 = me & 112, me & 14, me & 1
    ys = [((y2 + 2 * d) & 14) | (c1 ^ c) for d in (4, 5, 3, 6, 2, 7, 1, 0) for c in (1, 0)]

    def far_first(act):
        def ring(i, c):
            d = 4 + jnp.where((i & 1) == 1, -((i + 1) >> 1), i >> 1)
            zz = (z16 + 16 * d) & 112
            for y in ys:
                act(zz | y)
            return c
        lax.fori_loop(0, 7, ring, 0)
        for y in ys[:-1]:
            act(z16 | y)

    far_first(lambda j: pl.semaphore_signal(bar, inc=1, device_id={"bins": j}, device_id_type=MESH))
    for i in range(1, 4):
        pl.semaphore_signal(bar, inc=1, device_id={"scans": lax.rem(mx + i, 4)}, device_id_type=MESH)
    for ld in loads[1:]:
        ld.start()
    loads[0].wait()
    s1[EVEN, :] = jnp.transpose(x_v[0:128, :])
    s1[ODD, :] = jnp.transpose(x_v[128:256, :])
    pl.semaphore_wait(bar, ND + 2)

    def send_all(s, r, k, n=2):
        def one(j):
            pltpu.make_async_remote_copy(s.at[rows_of(j, n)], r.at[rows_of(me, n)], sem.at[k], sem.at[k + 1],
                                         device_id={"bins": j}, device_id_type=MESH).start()
        far_first(one)

    def wait_all(w, k):
        d = dummy.at[:, :, pl.ds(0, w)]
        pltpu.make_async_copy(d, d, sem.at[k]).wait()

    send_all(s1, r1, 0)
    r1[rows_of(me, 2), :] = s1[rows_of(me, 2), :]
    for ld in loads[1:]:
        ld.wait()
    T = twiddle(me)
    for i in range(4):
        t_v[i] = T[i]
    counts = cnt_v[...]
    for i, m in enumerate(onehots(starts_of(counts), me)):
        oh_v[i] = m.astype(F32)
    edges = [edges_v[i] for i in range(6)]
    t, band, occ = slot_info(counts, edges, me)
    sp_v[...] = state_part(prev_v[...], dyn_v, t, band)
    sel_v[...] = owner_select(t)
    wait_all(256, 1)
    wait_all(256, 0)

    s2[EVEN, :], s2[ODD, :] = stage1(jnp.concatenate([r1[EVEN, :], r1[ODD, :]], 1), (f1a_v[...], f1b_v[...], f1c_v[...]), (w2a_v[...], w2b_v[...], w2c_v[...]), tw_v)
    send_all(s2, r2, 2)
    r2[rows_of(me, 2), :] = s2[rows_of(me, 2), :]
    wait_all(256, 3)
    wait_all(256, 2)

    sums, y, E = stage2(jnp.concatenate([r2[EVEN, :], r2[ODD, :]], 1), me, [t_v[i] for i in range(4)], (mma_v[...], mmb_v[...], mmc_v[...]))
    xs[0:4, :] = sums[0:4, 0:128]
    xs[4:8, :] = sums[4:8, 128:256]
    for i in range(1, 4):
        pltpu.make_async_remote_copy(xs, xr.at[mx], sem.at[4], sem.at[5],
                                     device_id={"scans": lax.rem(mx + i, 4)}, device_id_type=MESH).start()
    xr[mx] = xs[...]
    S = [oh_v[i] > 0.5 for i in range(3)]
    Fr, Fi = stage2b(y, E, (mma_v[...], mmb_v[...], mmc_v[...]), g_v[...])
    mr, mi = stage3(Fr, Fi, E, S)
    mi = pltpu.roll(mi, 64, 1)
    d = xr.at[pl.ds(0, 3)]
    pltpu.make_async_copy(d, d, sem.at[5]).wait()
    pltpu.make_async_copy(d, d, sem.at[4]).wait()
    tot = xr[0] + xr[1] + xr[2] + xr[3]
    s3[...] = stage3b(mr, mi, S, tot)
    send_all(s3, r3, 6, 1)
    r3[pl.ds(me, 1), :] = s3[pl.ds(me, 1), :]
    wait_all(128, 7)
    wait_all(128, 6)
    t, band, occ = slot_info(cnt_v[...], edges, me)
    o_ref[...] = stage4(r3[...], sel_v[...], t, band, occ, pl_v[...], co_v[...], sp_v[...])


def emit(a_ref, o_ref, sem):
    c = pltpu.make_async_copy(a_ref, o_ref, sem)
    c.start()
    c.wait()


def body(profiles, band_edges, owner_counts, dynamics, prev_state):
    tb = tables()
    consts = [*tb["F1"], *tb["MM"], *tb["W2"], tb["tw"], tb["G"], tb["place"], tb["co"]]
    ins = [profiles.reshape(256, 128), owner_counts.reshape(1, 128), band_edges, dynamics, prev_state.reshape(64, 128)]
    ins += [jnp.asarray(c) for c in consts]
    V = pltpu.VMEM
    out = pl.pallas_call(
        kernel,
        out_shape=V((64, 128), F32),
        in_specs=[pl.BlockSpec(memory_space=pltpu.HBM)] * len(ins),
        out_specs=pl.BlockSpec(memory_space=V),
        scratch_shapes=[(pltpu.SMEM if i.shape == (6,) else V)(i.shape, i.dtype) for i in ins] + [
            *[V((256, 128), F32)] * 4, *[V((128, 128), F32)] * 2, V((8, 128), F32), V((4, 8, 128), F32),
            V((127, 1, 256), F32), V((4, 128, 128), F32), V((3, 128, 128), F32), V((64, 128), F32), V((320, 128), BF),
            pltpu.SemaphoreType.DMA((len(ins),)), pltpu.SemaphoreType.DMA((8,))],
        compiler_params=pltpu.CompilerParams(collective_id=0, has_side_effects=True, vmem_limit_bytes=48 << 20),
    )(*[pltpu.with_memory_space_constraint(i, pltpu.HBM) for i in ins])
    return out.reshape(64, 1, 128)


def solution(mesh):
    return jax.shard_map(
        body,
        mesh=mesh,
        in_specs=(P("scans", "bins"), P(), P(), P(), P("bins", "scans", None)),
        out_specs=P("bins", "scans", None),
        check_vma=False,
    )
```

```python
import functools

import jax
import jax.numpy as jnp
import ml_dtypes
import numpy as np
from jax import lax
from jax.experimental import pallas as pl
from jax.experimental.pallas import tpu as pltpu
from jax.sharding import PartitionSpec as P

MESH = pl.DeviceIdType.MESH
BF=jnp.bfloat16; F32=jnp.float32
ND=128; NB=1<<22; M=1<<15; EPS=1e-5; NCLASS=5

def triple(a):
    parts=[]
    for _ in range(3):
        parts.append(a.astype(np.float32).astype(ml_dtypes.bfloat16))
        a=a-parts[-1].astype(np.float64)
    return parts
def split(x):
    hi=x.astype(BF); lo=(x-hi.astype(F32)).astype(BF)
    return hi,lo
def dot(a,b): return lax.dot_general(a,b,(((1,),(0,)),((),())),preferred_element_type=F32)
def split3(x):
    p=x.astype(BF); r=x-p.astype(F32); q=r.astype(BF)
    return p,q,(r-q.astype(F32)).astype(BF)
def dot6(a,b,d=None):
    d=d or dot
    return d(a[0],b[0])+((d(a[0],b[1])+d(a[1],b[0]))+((d(a[0],b[2])+d(a[2],b[0]))+d(a[1],b[1])))
def dot6s(a,b,d=None):
    d=d or dot
    m=a.shape[0]//3
    p,q,t=d(a,b[0]),d(a[:2*m],b[1]),d(a[:m],b[2])
    return p[:m]+((q[:m]+p[m:2*m])+((t+p[2*m:])+q[m:]))
def dot_nt(a,b): return lax.dot_general(a,b,(((1,),(1,)),((),())),preferred_element_type=F32)
def dot3(a,b,d=dot):
    return d(a[0],b[0])+(d(a[0],b[1])+d(a[1],b[0]))
def tables():
    i=np.arange(128)[:,None]; j=np.arange(128)[None,:]; a=np.arange(256)[None,:]
    ang=2*np.pi*(i*j%128)/128; C,S=np.cos(ang),np.sin(ang)
    F1=np.concatenate([C,-S],0)
    MM=np.block([[C,S],[-S,C]])
    ang=2*np.pi*(i*a%256)/256; C2,S2=np.cos(ang),np.sin(ang)
    W2=np.block([[C2,S2]])
    ang=2*np.pi*(i*a)/M
    tw=np.stack([np.cos(ang),-np.sin(ang)]).astype(np.float32)
    b=np.arange(128)
    G=np.zeros((128,128))
    G[b,b//8]=1
    for m in range(16):
        g=15-m
        for bb in range(8*g+1,min(8*g+9,128)): G[bb,16+m]=1
    place=np.zeros((5,128,256))
    for q in range(5):
        for m in range(16):
            if q<4:
                place[q,m,16*q+m]=1; place[q,64+m,64+16*q+m]=1
                place[q,16+m,48-16*q+m]=1; place[q,80+m,64+48-16*q+m]=-1
        if q<4:
            place[q,40,128]=1; place[q,41,128]=1
        if q>=1:
            place[q,42,128]=1; place[q,32,64-16*q]=1; place[q,96,128-16*q]=-1
    place=place.reshape(640,256)
    co=np.zeros((5,128,128))
    for be in range(5):
        for k in range(64):
            co[be,k,k>>be]=1; co[be,64+k,64+(k>>be)]=1
    co=co.reshape(640,128)
    f0,f1,f2=triple(F1)
    return dict(F1=[np.block([[f0,f0],[f1,f1]]),np.concatenate([f0,f2],1)],MM=np.concatenate(triple(MM),0),W2=np.concatenate(triple(W2),0),tw=tw,G=np.concatenate([G,G],0).astype(ml_dtypes.bfloat16),place=place.astype(ml_dtypes.bfloat16),co=co.astype(ml_dtypes.bfloat16))

def iota(shape,d): return lax.broadcasted_iota(jnp.int32,shape,d)

def stage1(R1, F1, W2, tw):
    g0,g1,g2=split3(R1)
    g01=jnp.concatenate([g0,g1],0)
    A=dot(F1[0],g01)
    A=A[:256]+(A[256:]+dot(F1[1],jnp.concatenate([g2,g0],0)))
    Ar,Ai=A[:128],A[128:]
    tr,ti=tw[0],tw[1]
    Br=Ar*tr-Ai*ti; Bi=Ar*ti+Ai*tr
    rs,qs=split3(Br),split3(Bi)
    def both(r,i):
        return jnp.concatenate([jnp.concatenate([r,i],1),jnp.concatenate([i,-r],1)],0)
    Y=dot6s(W2, [both(r,i) for r,i in zip(rs,qs)], dot_nt)
    lane=iota((1,256),1)
    nyq=jnp.sum(jnp.where(lane%2==0,Br[0:1],-Br[0:1]),axis=1,keepdims=True)
    first=(iota((128,256),0)==0)&(iota((128,256),1)==128)
    Y=jnp.where(first,nyq,Y)
    return Y[:,:128],Y[:,128:]

def twiddle(me):
    n=iota((128,128),0); b=iota((128,128),1)
    th=(n*(128*me+b)).astype(F32)*(2*np.pi/NB)
    nn=n.astype(F32)*(2*np.pi/256)
    zero=me==0
    return jnp.cos(th),jnp.sin(th),jnp.cos(nn),jnp.sin(nn)

def stage2(R2, me, T, MM):
    Tr,Ts,Nr,Ns=T
    Rr,Ri=R2[:,:128],R2[:,128:]
    lane0=iota((128,128),1)==0
    zero=me==0
    Ri0=jnp.where(lane0&zero,0.0,Ri)
    Yr=Rr*Tr+Ri0*Ts; Yi=Ri0*Tr-Rr*Ts
    Er=jnp.where(zero,Ri*Nr,Yr); Ei=jnp.where(zero,-Ri*Ns,Yi)
    Y=jnp.concatenate([Yr,Yi],0); E=jnp.concatenate([Er,Ei],0)
    ys,es=split3(Y),split3(E)
    X=dot6s(MM,[jnp.concatenate([y,e],1) for y,e in zip(ys,es)])
    Xr,Xi,Er,Ei=X[:128,:128],X[128:,:128],X[:128,128:],X[128:,128:]
    rows=iota((128,128),0)
    Pw=jnp.where(lane0&(rows>=64),0.0,Xr*Xr+Xi*Xi)
    Pe=jnp.where(lane0,Er*Er+Ei*Ei,0.0)
    ph,pl_=split(jnp.concatenate([Pw,Pe],0))
    sums=dot_nt(jnp.ones((8,256),BF),jnp.concatenate([ph,pl_],1))
    return sums,ys,(Er,Ei)

def stage2b(y, E, MM, G):
    Z=dot(jnp.concatenate(y[:2],1),G)+dot(y[2],G[:128])
    F=dot6s(MM,split3(Z))
    return F[:128],F[128:]

def starts_of(counts_row):
    o=iota((128,128),0); k=iota((128,128),1)
    return jnp.sum(jnp.where(k<o,counts_row.astype(F32),0.0),axis=1,keepdims=True).astype(jnp.int32)

def onehots(starts, me):
    q4=me//4
    k=iota((128,128),1)
    def row(cl):
        return (starts+((cl-starts)&63))>>6
    main=row(q4); mir=127-row(63-q4); ext=127-row(63-((me+127)%128)//4)
    Sm=(k==main)&(k<64); Sx=(k==mir)&(k>=64); Se=(k==ext)&(k>=64)
    return Sm,Sx,Se

def stage3(Fr,Fi,E,S):
    Sm,Sx,Se=S
    rows=iota((128,128),0); lane=iota((128,128),1)
    keep=((rows<64)&(lane<16))|((rows>=64)&(lane>=16)&(lane<32))
    keepe=(rows>=64)&(lane==32)
    Wm=jnp.concatenate([jnp.where(keep,Fr,0.0),jnp.where(keep,Fi,0.0)],1)
    We=jnp.concatenate([jnp.where(keepe,E[0][:,0:1],0.0),jnp.where(keepe,E[1][:,0:1],0.0)],1)
    W=jnp.concatenate([Wm,We],0)
    SS=jnp.concatenate([(Sm|Sx).astype(F32).astype(BF),Se.astype(F32).astype(BF)],1)
    h,l=split(W)
    Ms=dot(SS,h)+dot(SS,l)
    return Ms[:,:128], Ms[:,128:]

def stage3b(mr,mi_rolled,S,tot):
    Sm,Sx,Se=S
    p0=tot[0:1]; p1=tot[4:5]
    z=0.0
    a=jnp.sum(jnp.where(Sm,p0,z),axis=1,keepdims=True)
    b=jnp.sum(jnp.where(Sx,p0,z),axis=1,keepdims=True)
    c=jnp.sum(jnp.where(Se,p1,z),axis=1,keepdims=True)
    lane=iota((128,128),1)
    return jnp.where(lane<40,mr,jnp.where(lane>=64,mi_rolled,jnp.where(lane==40,a,jnp.where(lane==41,b,jnp.where(lane==42,c,0.0)))))

def slot_info(counts_row, edges, me):
    k=iota((64,128),1)
    st=jnp.sum(jnp.where(k<me,counts_row.astype(F32),0.0),axis=1,keepdims=True).astype(jnp.int32)
    cn=jnp.sum(jnp.where(k==me,counts_row.astype(F32),0.0),axis=1,keepdims=True).astype(jnp.int32)
    s=iota((64,1),0)
    t=st+s
    band=sum([(t>=edges[e]).astype(jnp.int32) for e in range(1,5)])
    return t,band,s<cn

def owner_select(t):
    c=t&63; main=c<32
    j=iota((64,128),1)
    r4=4*jnp.where(main,c,63-c)
    sel=[(j==r4+q).astype(F32).astype(BF) for q in range(4)]
    sel.append((j==((4*(64-c))&127)).astype(F32).astype(BF))
    return jnp.concatenate(sel,0)

def state_part(prev, dyn, t, band):
    pr=jnp.concatenate([prev[:,:64],prev[:,64:]],0)
    band2=jnp.concatenate([band,band],0)
    cnt=64>>band2
    lane=iota((128,64),1)
    pr=jnp.where(lane<cnt,pr,0.0)
    out=jnp.zeros((128,64),F32)
    for be in range(NCLASS):
        x=jnp.where(band2==be,pr,0.0)
        out=out+dot6(split3(x),split3(dyn[be]),dot_nt)
    out=jnp.where(lane<cnt,out,0.0)
    return jnp.concatenate([out[:64],out[64:]],1)

def stage4(R3, sel, t, band, occ, place, co, spart):
    h,l=split(R3)
    main=(t&63)<32
    lane=iota((64,128),1)
    inmain=(lane<16)|((lane>=64)&(lane<80))|(lane==40)
    inmir=((lane>=16)&(lane<32))|((lane>=80)&(lane<96))|(lane==41)
    inext=(lane==32)|(lane==96)|(lane==42)
    T=dot(sel,jnp.concatenate([h,l],1))
    halves=[]
    for v in (T[:,:128],T[:,128:]):
        parts=[]
        for q in range(5):
            mk=(main&inmain&(q<4))|(jnp.logical_not(main)&((inmir&(q<4))|(inext&(q>=1))))
            parts.append(jnp.where(mk,v[64*q:64*q+64],0.0).astype(BF))
        halves.append(jnp.concatenate(parts,1))
    res=dot(jnp.concatenate(halves,0),place)
    res=res[:64]+res[64:]
    fine=res[:,:128]; pw=res[:,128:129]
    fhl=jnp.concatenate(split(fine),0).astype(F32)
    band2=jnp.concatenate([band,band],0)
    x=jnp.concatenate([jnp.where(band2==be,fhl,0.0).astype(BF) for be in range(5)],1)
    meas=dot(x,co)
    meas=meas[:64]+meas[64:]
    mp=pw/(4*512)
    scale=1.0/jnp.sqrt((8<<band).astype(F32)*(mp+EPS))
    st=iota((64,128),1)&63
    meas=jnp.where(st<(64>>band),meas*scale,0.0)
    return jnp.where(occ,meas+spart,0.0)


EVEN, ODD = pl.ds(0, 128, stride=2), pl.ds(1, 128, stride=2)


def rows_of(j, n):
    return pl.ds(pl.multiple_of(n * j, n), n)


def kernel(x_h, cnt_h, edges_h, dyn_h, prev_h, f1a_h, f1b_h, mm_h, w2_h, tw_h, g_h, pl_h, co_h,
           o_ref,
           x_v, cnt_v, edges_v, dyn_v, prev_v, f1a_v, f1b_v, mm_v, w2_v, tw_v, g_v, pl_v, co_v,
           s1, r1, s2, r2, s3, r3, xs, xr, dummy, t_v, oh_v, sp_v, sel_v, csem, sem):
    me = lax.axis_index("bins")
    mx = lax.axis_index("scans")
    hs = [x_h, cnt_h, edges_h, dyn_h, prev_h, f1a_h, f1b_h, mm_h, w2_h, tw_h, g_h, pl_h, co_h]
    vs = [x_v, cnt_v, edges_v, dyn_v, prev_v, f1a_v, f1b_v, mm_v, w2_v, tw_v, g_v, pl_v, co_v]
    loads = [pltpu.make_async_copy(h, v, csem.at[i]) for i, (h, v) in enumerate(zip(hs, vs))]
    loads[0].start()
    bar = pltpu.get_barrier_semaphore()

    z16, y2, c1 = me & 112, me & 14, me & 1
    ys = [((y2 + 2 * d) & 14) | (c1 ^ c) for d in (4, 5, 3, 6, 2, 7, 1, 0) for c in (1, 0)]

    def far_first(act):
        def ring(i, c):
            d = 4 + jnp.where((i & 1) == 1, -((i + 1) >> 1), i >> 1)
            zz = (z16 + 16 * d) & 112
            for y in ys:
                act(zz | y)
            return c
        lax.fori_loop(0, 7, ring, 0)
        for y in ys[:-1]:
            act(z16 | y)

    far_first(lambda j: pl.semaphore_signal(bar, inc=1, device_id={"bins": j}, device_id_type=MESH))
    for i in range(1, 4):
        pl.semaphore_signal(bar, inc=1, device_id={"scans": lax.rem(mx + i, 4)}, device_id_type=MESH)
    for ld in loads[1:]:
        ld.start()
    loads[0].wait()
    s1[EVEN, :] = jnp.transpose(x_v[0:128, :])
    s1[ODD, :] = jnp.transpose(x_v[128:256, :])
    pl.semaphore_wait(bar, ND + 2)

    def send_all(s, r, k, n=2):
        def one(j):
            pltpu.make_async_remote_copy(s.at[rows_of(j, n)], r.at[rows_of(me, n)], sem.at[k], sem.at[k + 1],
                                         device_id={"bins": j}, device_id_type=MESH).start()
        far_first(one)

    def wait_all(w, k):
        d = dummy.at[:, :, pl.ds(0, w)]
        pltpu.make_async_copy(d, d, sem.at[k]).wait()

    send_all(s1, r1, 0)
    r1[rows_of(me, 2), :] = s1[rows_of(me, 2), :]
    for ld in loads[1:]:
        ld.wait()
    T = twiddle(me)
    for i in range(4):
        t_v[i] = T[i]
    counts = cnt_v[...]
    for i, m in enumerate(onehots(starts_of(counts), me)):
        oh_v[i] = m.astype(F32)
    edges = [edges_v[i] for i in range(6)]
    t, band, occ = slot_info(counts, edges, me)
    sp_v[...] = state_part(prev_v[...], dyn_v, t, band)
    sel_v[...] = owner_select(t)
    wait_all(256, 1)
    wait_all(256, 0)

    s2[EVEN, :], s2[ODD, :] = stage1(jnp.concatenate([r1[EVEN, :], r1[ODD, :]], 1), (f1a_v[...], f1b_v[...]), w2_v[...], tw_v)
    send_all(s2, r2, 2)
    r2[rows_of(me, 2), :] = s2[rows_of(me, 2), :]
    wait_all(256, 3)
    wait_all(256, 2)

    sums, y, E = stage2(jnp.concatenate([r2[EVEN, :], r2[ODD, :]], 1), me, [t_v[i] for i in range(4)], mm_v[...])
    xs[0:4, :] = sums[0:4, 0:128]
    xs[4:8, :] = sums[4:8, 128:256]
    for i in range(1, 4):
        pltpu.make_async_remote_copy(xs, xr.at[mx], sem.at[4], sem.at[5],
                                     device_id={"scans": lax.rem(mx + i, 4)}, device_id_type=MESH).start()
    xr[mx] = xs[...]
    S = [oh_v[i] > 0.5 for i in range(3)]
    Fr, Fi = stage2b(y, E, mm_v[...], g_v[...])
    mr, mi = stage3(Fr, Fi, E, S)
    mi = pltpu.roll(mi, 64, 1)
    d = xr.at[pl.ds(0, 3)]
    pltpu.make_async_copy(d, d, sem.at[5]).wait()
    pltpu.make_async_copy(d, d, sem.at[4]).wait()
    tot = xr[0] + xr[1] + xr[2] + xr[3]
    s3[...] = stage3b(mr, mi, S, tot)
    send_all(s3, r3, 6, 1)
    r3[pl.ds(me, 1), :] = s3[pl.ds(me, 1), :]
    wait_all(128, 7)
    wait_all(128, 6)
    t, band, occ = slot_info(cnt_v[...], edges, me)
    o_ref[...] = stage4(r3[...], sel_v[...], t, band, occ, pl_v[...], co_v[...], sp_v[...])


def emit(a_ref, o_ref, sem):
    c = pltpu.make_async_copy(a_ref, o_ref, sem)
    c.start()
    c.wait()


def body(profiles, band_edges, owner_counts, dynamics, prev_state):
    tb = tables()
    consts = [*tb["F1"], tb["MM"], tb["W2"], tb["tw"], tb["G"], tb["place"], tb["co"]]
    ins = [profiles.reshape(256, 128), owner_counts.reshape(1, 128), band_edges, dynamics, prev_state.reshape(64, 128)]
    ins += [jnp.asarray(c) for c in consts]
    V = pltpu.VMEM
    out = pl.pallas_call(
        kernel,
        out_shape=V((64, 128), F32),
        in_specs=[pl.BlockSpec(memory_space=pltpu.HBM)] * len(ins),
        out_specs=pl.BlockSpec(memory_space=V),
        scratch_shapes=[(pltpu.SMEM if i.shape == (6,) else V)(i.shape, i.dtype) for i in ins] + [
            *[V((256, 128), F32)] * 4, *[V((128, 128), F32)] * 2, V((8, 128), F32), V((4, 8, 128), F32),
            V((127, 1, 256), F32), V((4, 128, 128), F32), V((3, 128, 128), F32), V((64, 128), F32), V((320, 128), BF),
            pltpu.SemaphoreType.DMA((len(ins),)), pltpu.SemaphoreType.DMA((8,))],
        compiler_params=pltpu.CompilerParams(collective_id=0, has_side_effects=True, vmem_limit_bytes=48 << 20),
    )(*[pltpu.with_memory_space_constraint(i, pltpu.HBM) for i in ins])
    return out.reshape(64, 1, 128)


def solution(mesh):
    return jax.shard_map(
        body,
        mesh=mesh,
        in_specs=(P("scans", "bins"), P(), P(), P(), P("bins", "scans", None)),
        out_specs=P("bins", "scans", None),
        check_vma=False,
    )
```

```python
import functools

import jax
import jax.numpy as jnp
import ml_dtypes
import numpy as np
from jax import lax
from jax.experimental import pallas as pl
from jax.experimental.pallas import tpu as pltpu
from jax.sharding import PartitionSpec as P

MESH = pl.DeviceIdType.MESH
BF=jnp.bfloat16; F32=jnp.float32
ND=128; NB=1<<22; M=1<<15; EPS=1e-5; NCLASS=5

def triple(a):
    parts=[]
    for _ in range(3):
        parts.append(a.astype(np.float32).astype(ml_dtypes.bfloat16))
        a=a-parts[-1].astype(np.float64)
    return parts
def split(x):
    hi=x.astype(BF); lo=(x-hi.astype(F32)).astype(BF)
    return hi,lo
def dot(a,b): return lax.dot_general(a,b,(((1,),(0,)),((),())),preferred_element_type=F32)
def split3(x):
    p=x.astype(BF); r=x-p.astype(F32); q=r.astype(BF)
    return p,q,(r-q.astype(F32)).astype(BF)
def dot6(a,b,d=None):
    d=d or dot
    return d(a[0],b[0])+((d(a[0],b[1])+d(a[1],b[0]))+((d(a[0],b[2])+d(a[2],b[0]))+d(a[1],b[1])))
def dot6s(a,b,d=None):
    d=d or dot
    m=a.shape[0]//3
    p,q,t=d(a,b[0]),d(a[:2*m],b[1]),d(a[:m],b[2])
    return p[:m]+((q[:m]+p[m:2*m])+((t+p[2*m:])+q[m:]))
def dot_nt(a,b): return lax.dot_general(a,b,(((1,),(1,)),((),())),preferred_element_type=F32)
def dot3(a,b,d=dot):
    return d(a[0],b[0])+(d(a[0],b[1])+d(a[1],b[0]))
def tables():
    i=np.arange(128)[:,None]; j=np.arange(128)[None,:]; a=np.arange(256)[None,:]
    ang=2*np.pi*(i*j%128)/128; C,S=np.cos(ang),np.sin(ang)
    F1=np.concatenate([C,-S],0)
    MM=np.block([[C,S],[-S,C]])
    ang=2*np.pi*(i*a%256)/256; C2,S2=np.cos(ang),np.sin(ang)
    W2=np.block([[C2,S2]])
    ang=2*np.pi*(i*a)/M
    tw=np.stack([np.cos(ang),-np.sin(ang)]).astype(np.float32)
    b=np.arange(128)
    G=np.zeros((128,128))
    G[b,b//8]=1
    for m in range(16):
        g=15-m
        for bb in range(8*g+1,min(8*g+9,128)): G[bb,16+m]=1
    place=np.zeros((5,128,256))
    for q in range(5):
        for m in range(16):
            if q<4:
                place[q,m,16*q+m]=1; place[q,64+m,64+16*q+m]=1
                place[q,16+m,48-16*q+m]=1; place[q,80+m,64+48-16*q+m]=-1
        if q<4:
            place[q,40,128]=1; place[q,41,128]=1
        if q>=1:
            place[q,42,128]=1; place[q,32,64-16*q]=1; place[q,96,128-16*q]=-1
    place=place.reshape(640,256)
    co=np.zeros((5,128,128))
    for be in range(5):
        for k in range(64):
            co[be,k,k>>be]=1; co[be,64+k,64+(k>>be)]=1
    co=co.reshape(640,128)
    f0,f1,f2=triple(F1)
    return dict(F1=[np.block([[f0,f0],[f1,f1]]),np.concatenate([f0,f2],1)],MM=np.concatenate(triple(MM),0),W2=np.concatenate(triple(W2),0),tw=tw,G=np.concatenate([G,G],0).astype(ml_dtypes.bfloat16),place=place.astype(ml_dtypes.bfloat16),co=co.astype(ml_dtypes.bfloat16))

def iota(shape,d): return lax.broadcasted_iota(jnp.int32,shape,d)

def stage1(R1, F1, W2, tw):
    g0,g1,g2=split3(R1)
    g01=jnp.concatenate([g0,g1],0)
    A=dot(F1[0],g01)
    A=A[:256]+(A[256:]+dot(F1[1],jnp.concatenate([g2,g0],0)))
    Ar,Ai=A[:128],A[128:]
    tr,ti=tw[0],tw[1]
    Br=Ar*tr-Ai*ti; Bi=Ar*ti+Ai*tr
    rs,qs=split3(Br),split3(Bi)
    def both(r,i):
        return jnp.concatenate([jnp.concatenate([r,i],1),jnp.concatenate([i,-r],1)],0)
    Y=dot6s(W2, [both(r,i) for r,i in zip(rs,qs)], dot_nt)
    lane=iota((1,256),1)
    nyq=jnp.sum(jnp.where(lane%2==0,Br[0:1],-Br[0:1]),axis=1,keepdims=True)
    first=(iota((128,256),0)==0)&(iota((128,256),1)==128)
    Y=jnp.where(first,nyq,Y)
    return Y[:,:128],Y[:,128:]

def twiddle(me):
    n=iota((128,128),0); b=iota((128,128),1)
    th=(n*(128*me+b)).astype(F32)*(2*np.pi/NB)
    nn=n.astype(F32)*(2*np.pi/256)
    zero=me==0
    return jnp.cos(th),jnp.sin(th),jnp.cos(nn),jnp.sin(nn)

def stage2(R2, me, T, MM):
    Tr,Ts,Nr,Ns=T
    Rr,Ri=R2[:,:128],R2[:,128:]
    lane0=iota((128,128),1)==0
    zero=me==0
    Ri0=jnp.where(lane0&zero,0.0,Ri)
    Yr=Rr*Tr+Ri0*Ts; Yi=Ri0*Tr-Rr*Ts
    Er=jnp.where(zero,Ri*Nr,Yr); Ei=jnp.where(zero,-Ri*Ns,Yi)
    Y=jnp.concatenate([Yr,Yi],0); E=jnp.concatenate([Er,Ei],0)
    ys,es=split3(Y),split3(E)
    X=dot6s(MM,[jnp.concatenate([y,e],1) for y,e in zip(ys,es)])
    Xr,Xi,Er,Ei=X[:128,:128],X[128:,:128],X[:128,128:],X[128:,128:]
    rows=iota((128,128),0)
    Pw=jnp.where(lane0&(rows>=64),0.0,Xr*Xr+Xi*Xi)
    Pe=jnp.where(lane0,Er*Er+Ei*Ei,0.0)
    ph,pl_=split(jnp.concatenate([Pw,Pe],0))
    sums=dot_nt(jnp.ones((8,256),BF),jnp.concatenate([ph,pl_],1))
    return sums,ys,(Er,Ei)

def stage2b(y, E, MM, G):
    Z=dot(jnp.concatenate(y[:2],1),G)+dot(y[2],G[:128])
    F=dot6s(MM,split3(Z))
    return F[:128],F[128:]

def starts_of(counts_row):
    o=iota((128,128),0); k=iota((128,128),1)
    return jnp.sum(jnp.where(k<o,counts_row.astype(F32),0.0),axis=1,keepdims=True).astype(jnp.int32)

def onehots(starts, me):
    q4=me//4
    k=iota((128,128),1)
    def row(cl):
        return (starts+((cl-starts)&63))>>6
    main=row(q4); mir=127-row(63-q4); ext=127-row(63-((me+127)%128)//4)
    Sm=(k==main)&(k<64); Sx=(k==mir)&(k>=64); Se=(k==ext)&(k>=64)
    return Sm,Sx,Se

def stage3(Fr,Fi,E,S):
    Sm,Sx,Se=S
    rows=iota((128,128),0); lane=iota((128,128),1)
    keep=((rows<64)&(lane<16))|((rows>=64)&(lane>=16)&(lane<32))
    keepe=(rows>=64)&(lane==32)
    Wm=jnp.concatenate([jnp.where(keep,Fr,0.0),jnp.where(keep,Fi,0.0)],1)
    We=jnp.concatenate([jnp.where(keepe,E[0][:,0:1],0.0),jnp.where(keepe,E[1][:,0:1],0.0)],1)
    W=jnp.concatenate([Wm,We],0)
    SS=jnp.concatenate([(Sm|Sx).astype(F32).astype(BF),Se.astype(F32).astype(BF)],1)
    h,l=split(W)
    Ms=dot(SS,h)+dot(SS,l)
    return Ms[:,:128], Ms[:,128:]

def stage3b(mr,mi_rolled,S,tot):
    Sm,Sx,Se=S
    p0=tot[0:1]; p1=tot[4:5]
    z=0.0
    a=jnp.sum(jnp.where(Sm,p0,z),axis=1,keepdims=True)
    b=jnp.sum(jnp.where(Sx,p0,z),axis=1,keepdims=True)
    c=jnp.sum(jnp.where(Se,p1,z),axis=1,keepdims=True)
    lane=iota((128,128),1)
    return jnp.where(lane<40,mr,jnp.where(lane>=64,mi_rolled,jnp.where(lane==40,a,jnp.where(lane==41,b,jnp.where(lane==42,c,0.0)))))

def slot_info(counts_row, edges, me):
    k=iota((64,128),1)
    st=jnp.sum(jnp.where(k<me,counts_row.astype(F32),0.0),axis=1,keepdims=True).astype(jnp.int32)
    cn=jnp.sum(jnp.where(k==me,counts_row.astype(F32),0.0),axis=1,keepdims=True).astype(jnp.int32)
    s=iota((64,1),0)
    t=st+s
    band=sum([(t>=edges[e]).astype(jnp.int32) for e in range(1,5)])
    return t,band,s<cn

def owner_select(t):
    c=t&63; main=c<32
    j=iota((64,128),1)
    r4=4*jnp.where(main,c,63-c)
    sel=[(j==r4+q).astype(F32).astype(BF) for q in range(4)]
    sel.append((j==((4*(64-c))&127)).astype(F32).astype(BF))
    return jnp.concatenate(sel,0)

def state_part(prev, dyn, t, band):
    pr=jnp.concatenate([prev[:,:64],prev[:,64:]],0)
    band2=jnp.concatenate([band,band],0)
    cnt=64>>band2
    lane=iota((128,64),1)
    pr=jnp.where(lane<cnt,pr,0.0)
    out=jnp.zeros((128,64),F32)
    for be in range(NCLASS):
        x=jnp.where(band2==be,pr,0.0)
        out=out+dot6(split3(x),split3(dyn[be]),dot_nt)
    out=jnp.where(lane<cnt,out,0.0)
    return jnp.concatenate([out[:64],out[64:]],1)

def stage4(R3, sel, t, band, occ, place, co, spart):
    h,l=split(R3)
    main=(t&63)<32
    lane=iota((64,128),1)
    inmain=(lane<16)|((lane>=64)&(lane<80))|(lane==40)
    inmir=((lane>=16)&(lane<32))|((lane>=80)&(lane<96))|(lane==41)
    inext=(lane==32)|(lane==96)|(lane==42)
    T=dot(sel,jnp.concatenate([h,l],1))
    halves=[]
    for v in (T[:,:128],T[:,128:]):
        parts=[]
        for q in range(5):
            mk=(main&inmain&(q<4))|(jnp.logical_not(main)&((inmir&(q<4))|(inext&(q>=1))))
            parts.append(jnp.where(mk,v[64*q:64*q+64],0.0).astype(BF))
        halves.append(jnp.concatenate(parts,1))
    res=dot(jnp.concatenate(halves,0),place)
    res=res[:64]+res[64:]
    fine=res[:,:128]; pw=res[:,128:129]
    fhl=jnp.concatenate(split(fine),0).astype(F32)
    band2=jnp.concatenate([band,band],0)
    x=jnp.concatenate([jnp.where(band2==be,fhl,0.0).astype(BF) for be in range(5)],1)
    meas=dot(x,co)
    meas=meas[:64]+meas[64:]
    mp=pw/(4*512)
    scale=1.0/jnp.sqrt((8<<band).astype(F32)*(mp+EPS))
    st=iota((64,128),1)&63
    meas=jnp.where(st<(64>>band),meas*scale,0.0)
    return jnp.where(occ,meas+spart,0.0)


EVEN, ODD = pl.ds(0, 128, stride=2), pl.ds(1, 128, stride=2)


def rows_of(j, n):
    return pl.ds(pl.multiple_of(n * j, n), n)


def kernel(x_h, cnt_h, edges_h, dyn_h, prev_h, f1a_h, f1b_h, mm_h, w2_h, tw_h, g_h, pl_h, co_h,
           o_ref,
           x_v, cnt_v, edges_v, dyn_v, prev_v, f1a_v, f1b_v, mm_v, w2_v, tw_v, g_v, pl_v, co_v,
           s1, r1, s2, r2, s3, r3, xs, xr, dummy, t_v, oh_v, sp_v, sel_v, csem, sem):
    me = lax.axis_index("bins")
    mx = lax.axis_index("scans")
    hs = [x_h, cnt_h, edges_h, dyn_h, prev_h, f1a_h, f1b_h, mm_h, w2_h, tw_h, g_h, pl_h, co_h]
    vs = [x_v, cnt_v, edges_v, dyn_v, prev_v, f1a_v, f1b_v, mm_v, w2_v, tw_v, g_v, pl_v, co_v]
    loads = [pltpu.make_async_copy(h, v, csem.at[i]) for i, (h, v) in enumerate(zip(hs, vs))]
    loads[0].start()
    bar = pltpu.get_barrier_semaphore()

    z16, y2, c1 = me & 112, me & 14, me & 1
    ys = [((y2 + 2 * d) & 14) | (c1 ^ c) for d in (4, 5, 3, 6, 2, 7, 1, 0) for c in (1, 0)]

    def far_first(act):
        def ring(i, c):
            d = 4 + jnp.where((i & 1) == 1, -((i + 1) >> 1), i >> 1)
            zz = (z16 + 16 * d) & 112
            for y in ys:
                act(zz | y)
            return c
        lax.fori_loop(0, 7, ring, 0)
        for y in ys[:-1]:
            act(z16 | y)

    for i in range(1, 4):
        pl.semaphore_signal(bar, inc=1, device_id={"scans": lax.rem(mx + i, 4)}, device_id_type=MESH)
    far_first(lambda j: pl.semaphore_signal(bar, inc=1, device_id={"bins": j}, device_id_type=MESH))
    for ld in loads[1:]:
        ld.start()
    loads[0].wait()
    s1[EVEN, :] = jnp.transpose(x_v[0:128, :])
    s1[ODD, :] = jnp.transpose(x_v[128:256, :])
    pl.semaphore_wait(bar, ND + 2)

    def send_all(s, r, k, n=2):
        def one(j):
            pltpu.make_async_remote_copy(s.at[rows_of(j, n)], r.at[rows_of(me, n)], sem.at[k], sem.at[k + 1],
                                         device_id={"bins": j}, device_id_type=MESH).start()
        far_first(one)

    def wait_all(w, k):
        d = dummy.at[:, :, pl.ds(0, w)]
        pltpu.make_async_copy(d, d, sem.at[k]).wait()

    send_all(s1, r1, 0)
    r1[rows_of(me, 2), :] = s1[rows_of(me, 2), :]
    for ld in loads[1:]:
        ld.wait()
    T = twiddle(me)
    for i in range(4):
        t_v[i] = T[i]
    counts = cnt_v[...]
    for i, m in enumerate(onehots(starts_of(counts), me)):
        oh_v[i] = m.astype(F32)
    edges = [edges_v[i] for i in range(6)]
    t, band, occ = slot_info(counts, edges, me)
    sp_v[...] = state_part(prev_v[...], dyn_v, t, band)
    sel_v[...] = owner_select(t)
    wait_all(256, 1)
    wait_all(256, 0)

    s2[EVEN, :], s2[ODD, :] = stage1(jnp.concatenate([r1[EVEN, :], r1[ODD, :]], 1), (f1a_v[...], f1b_v[...]), w2_v[...], tw_v)
    send_all(s2, r2, 2)
    r2[rows_of(me, 2), :] = s2[rows_of(me, 2), :]
    wait_all(256, 3)
    wait_all(256, 2)

    sums, y, E = stage2(jnp.concatenate([r2[EVEN, :], r2[ODD, :]], 1), me, [t_v[i] for i in range(4)], mm_v[...])
    xs[0:4, :] = sums[0:4, 0:128]
    xs[4:8, :] = sums[4:8, 128:256]
    for i in range(1, 4):
        pltpu.make_async_remote_copy(xs, xr.at[mx], sem.at[4], sem.at[5],
                                     device_id={"scans": lax.rem(mx + i, 4)}, device_id_type=MESH).start()
    xr[mx] = xs[...]
    S = [oh_v[i] > 0.5 for i in range(3)]
    Fr, Fi = stage2b(y, E, mm_v[...], g_v[...])
    mr, mi = stage3(Fr, Fi, E, S)
    mi = pltpu.roll(mi, 64, 1)
    d = xr.at[pl.ds(0, 3)]
    pltpu.make_async_copy(d, d, sem.at[5]).wait()
    pltpu.make_async_copy(d, d, sem.at[4]).wait()
    tot = xr[0] + xr[1] + xr[2] + xr[3]
    s3[...] = stage3b(mr, mi, S, tot)
    send_all(s3, r3, 6, 1)
    r3[pl.ds(me, 1), :] = s3[pl.ds(me, 1), :]
    wait_all(128, 7)
    wait_all(128, 6)
    t, band, occ = slot_info(cnt_v[...], edges, me)
    o_ref[...] = stage4(r3[...], sel_v[...], t, band, occ, pl_v[...], co_v[...], sp_v[...])


def emit(a_ref, o_ref, sem):
    c = pltpu.make_async_copy(a_ref, o_ref, sem)
    c.start()
    c.wait()


def body(profiles, band_edges, owner_counts, dynamics, prev_state):
    tb = tables()
    consts = [*tb["F1"], tb["MM"], tb["W2"], tb["tw"], tb["G"], tb["place"], tb["co"]]
    ins = [profiles.reshape(256, 128), owner_counts.reshape(1, 128), band_edges, dynamics, prev_state.reshape(64, 128)]
    ins += [jnp.asarray(c) for c in consts]
    V = pltpu.VMEM
    out = pl.pallas_call(
        kernel,
        out_shape=V((64, 128), F32),
        in_specs=[pl.BlockSpec(memory_space=pltpu.HBM)] * len(ins),
        out_specs=pl.BlockSpec(memory_space=V),
        scratch_shapes=[(pltpu.SMEM if i.shape == (6,) else V)(i.shape, i.dtype) for i in ins] + [
            *[V((256, 128), F32)] * 4, *[V((128, 128), F32)] * 2, V((8, 128), F32), V((4, 8, 128), F32),
            V((127, 1, 256), F32), V((4, 128, 128), F32), V((3, 128, 128), F32), V((64, 128), F32), V((320, 128), BF),
            pltpu.SemaphoreType.DMA((len(ins),)), pltpu.SemaphoreType.DMA((8,))],
        compiler_params=pltpu.CompilerParams(collective_id=0, has_side_effects=True, vmem_limit_bytes=48 << 20),
    )(*[pltpu.with_memory_space_constraint(i, pltpu.HBM) for i in ins])
    return out.reshape(64, 1, 128)


def solution(mesh):
    return jax.shard_map(
        body,
        mesh=mesh,
        in_specs=(P("scans", "bins"), P(), P(), P(), P("bins", "scans", None)),
        out_specs=P("bins", "scans", None),
        check_vma=False,
    )
```
